32 devices in a mesh: groups: 2 (over x), frame: 16 (over z, y, core).
Axes of the slice: x: 2, y: 2, z: 4, core: 2. Of those that a mesh axis runs over, the one named last changes fastest.
Arguments:
- latent: bfloat16 [128, 32, 1152], P(('groups', 'frame')), parts along dimension 0, may hold values from -6 to 6
- ln_gain: float32 [1152], replicated, may hold values from 0.1 to 1.9
- q_gain: float32 [72], replicated, may hold values from 0.1 to 1.9
- k_gain: float32 [72], replicated, may hold values from 0.1 to 1.9
- w_qkv: bfloat16 [1152, 3456], replicated, may hold values from -0.1875 to 0.1875
- w_out: bfloat16 [1152, 1152], replicated, may hold values from -0.5 to 0.5
Outputs:
- result: bfloat16 [128, 32, 1152], P(('groups', 'frame')), parts along dimension 0
The draws below stay inside these ranges and needn't reach their ends.
There are 2 independent parts, one for each index of `groups`. The reference program is written for one: setup_inputs(seed, part) draws one part's arguments, and reference() takes and returns one part's arrays. A program takes and returns all parts, laid end to end along the dimension named above; an argument that names none is the same for every part. Nothing has to cross between parts.
All inputs are finite; a program needn't handle non-finite values.
Results may differ from the reference program's by a relative error of at most 0.006.
Values may be sent and summed in bfloat16 or wider, within the bound.
A program may use at most 64 MiB of HBM per device.

```python
import jax
import jax.numpy as jnp
from jax import lax

D = 1152
HEADS = 16
HEAD_DIM = 72
LAT_W = 32
WIN_ROWS = 4
FRAMES = 16


def block_levels(own_key, extent, shards, smallest, top_value):
    def one(axis_at, parts):
        steps = jax.random.uniform(jax.random.fold_in(jax.random.fold_in(own_key, 6), axis_at), (parts,), jnp.float32, smallest / len(shards), top_value / len(shards))
        return jnp.repeat(jnp.exp(steps), extent[axis_at] // parts).reshape((-1,) + (1,) * (len(extent) - axis_at - 1))

    level = one(*shards[0])
    for cut in shards[1:]:
        level = level * one(*cut)
    return level


def gaussian(own_key, shape, scale, limit, split=(), held_as=jnp.bfloat16):
    values = scale * jax.random.normal(own_key, shape, jnp.float32)
    if split:
        values = values * block_levels(own_key, shape, split, -0.22, 0.18)
    return jnp.clip(values, -limit, limit).astype(held_as)


def setup_inputs(seed: int = 0, part: int = 0) -> dict:
    arg_keys = jax.random.split(jax.random.key(seed), 7)
    part_splits = jax.random.split(jax.random.fold_in(arg_keys[6], part), 7)
    return {
        "latent": gaussian(part_splits[0], (FRAMES * WIN_ROWS, LAT_W, D), 1.0, 6.0, ((0, 16),)),
        "ln_gain": jnp.clip(1.0 + 0.18 * jax.random.normal(arg_keys[1], (D,), jnp.float32), 0.1, 1.9),
        "q_gain": jnp.clip(1.0 + 0.18 * jax.random.normal(arg_keys[2], (HEAD_DIM,), jnp.float32), 0.1, 1.9),
        "k_gain": jnp.clip(1.0 + 0.18 * jax.random.normal(arg_keys[3], (HEAD_DIM,), jnp.float32), 0.1, 1.9),
        "w_qkv": gaussian(arg_keys[4], (D, 3 * D), D ** -0.5, 0.1875),
        "w_out": gaussian(arg_keys[5], (D, D), (D // 8) ** -0.5, 0.5),
    }


def layer_norm(rows, ln_gain):
    values = rows.astype(jnp.float32)
    center = values - lax.optimization_barrier(jnp.mean(values, axis=-1, keepdims=True))
    spread = lax.optimization_barrier(jnp.mean(center * center, axis=-1, keepdims=True))
    return (center * lax.rsqrt(spread + 1e-06) * ln_gain).astype(jnp.bfloat16)

def head_norm(values, gain):
    shaped = values.reshape(values.shape[:-1] + (HEADS, HEAD_DIM))
    mean_sq = lax.optimization_barrier(jnp.mean(shaped * shaped, axis=-1, keepdims=True))
    return (shaped * lax.rsqrt(mean_sq + 1e-06) * gain).astype(jnp.bfloat16).reshape(values.shape)

def project(normed, w_qkv, q_gain, k_gain):
    width = normed.shape[-1]
    mixed = jnp.dot(normed.reshape(-1, width), w_qkv, preferred_element_type=jnp.float32)
    mixed = mixed.reshape(normed.shape[:-1] + (3 * width,))
    query = head_norm(mixed[..., :width], q_gain)
    keys = head_norm(mixed[..., width:2 * width], k_gain)
    values = mixed[..., 2 * width:].astype(jnp.bfloat16)
    return (query, keys, values)

def attend(query, keys, values):
    lead = query.shape[0]
    others = query.shape[1]
    q_four = query.reshape(lead, others, HEADS, HEAD_DIM).astype(jnp.float32)
    k_four = keys.reshape(lead, others, HEADS, HEAD_DIM).astype(jnp.float32)
    v_four = values.reshape(lead, others, HEADS, HEAD_DIM).astype(jnp.float32)
    scores = jnp.einsum('tshe,ushe->shtu', q_four, k_four) * HEAD_DIM ** (-0.5)
    weights = jnp.exp(scores)
    weights = (weights / lax.optimization_barrier(jnp.sum(weights, axis=-1, keepdims=True))).astype(jnp.bfloat16)
    mixed = jnp.einsum('shtu,ushe->tshe', weights.astype(jnp.float32), v_four)
    return mixed.astype(jnp.bfloat16).reshape(query.shape)

def reference(latent, ln_gain, q_gain, k_gain, w_qkv, w_out):
    frame_count = latent.shape[0] // WIN_ROWS
    grid = latent.reshape(frame_count, WIN_ROWS, LAT_W, D)

    def one_row(slab):
        normed = layer_norm(slab, ln_gain)
        query, keys, values = project(normed, w_qkv, q_gain, k_gain)
        mixed = attend(query, keys, values)
        branch = jnp.dot(mixed.reshape(-1, D), w_out, preferred_element_type=jnp.float32)
        return (slab.astype(jnp.float32) + branch.reshape(slab.shape)).astype(jnp.bfloat16)
    result = lax.map(one_row, jnp.swapaxes(grid, 0, 1))
    return jnp.swapaxes(result, 0, 1).reshape(latent.shape)
```

```python
import functools

import jax
import jax.numpy as jnp
from jax import lax
from jax.experimental import pallas as pl
from jax.experimental.pallas import tpu as pltpu
from jax.sharding import PartitionSpec as P

HEADS = 16
HEAD_DIM = 72
LANES = 128
WINDOW = 256
CHUNKS = 2
MID_CUTS = (0, 640, 1152)
OUT_CUTS = (0, 512, 1152)
PAIR_CUTS = (0, 4, 8)
STEP = 256
VMEM_BYTES = 30000000
MESH = pl.DeviceIdType.MESH
F32 = jnp.float32
BF16 = jnp.bfloat16
LOG2_E = 1.4426950408889634


def kernel(
    n,
    lat_hbm,
    ln_hbm,
    qg_hbm,
    kg_hbm,
    wq_hbm,
    wo_hbm,
    out_ref,
    lat,
    ln_ref,
    qg_ref,
    kg_ref,
    xs,
    xr,
    ys,
    yr,
    wq0,
    wq1,
    wo,
    acc,
    key_sum,
    query_sum,
    ones,
    lat_sem,
    gain_sem,
    wq_sem,
    wo_sem,
    s1,
    r1,
    s2,
    r2,
):
    rows, columns, model = lat_hbm.shape
    places = rows * columns // (n * CHUNKS)
    tokens = n * places
    half_rows = rows // CHUNKS
    groups = len(MID_CUTS) - 1
    pairs = HEADS // 2
    me = lax.axis_index("frame")
    side = lax.div(me, n // 2)
    spot = lax.rem(me, n // 2)
    far = (1 - side) * (n // 2)
    near = side * (n // 2)
    peers = [far + lax.rem(spot + k, n // 2) for k in range(n // 2)]
    peers += [near + lax.rem(spot + k, n // 2) for k in range(1, n // 2)]

    barrier = pltpu.get_barrier_semaphore()
    for to in peers:
        pl.semaphore_signal(barrier, inc=1, device_id={"frame": to}, device_id_type=MESH)

    lat_loads = []
    for c in range(CHUNKS):
        part = pl.ds(c * half_rows, half_rows)
        lat_loads.append(pltpu.make_async_copy(lat_hbm.at[part], lat.at[part], lat_sem.at[c]))
        lat_loads[-1].start()
    gains = [
        pltpu.make_async_copy(src, dst, gain_sem.at[i])
        for i, (src, dst) in enumerate(((ln_hbm, ln_ref), (qg_hbm, qg_ref), (kg_hbm, kg_ref)))
    ]
    for load in gains:
        load.start()
    wq_parts = (wq0, wq1)
    wq_loads = []
    for g in range(groups):
        a, b = MID_CUTS[g], MID_CUTS[g + 1]
        for third in range(3):
            load = pltpu.make_async_copy(
                wq_hbm.at[:, pl.ds(third * model + a, b - a)],
                wq_parts[g].at[:, pl.ds(third * (b - a), b - a)],
                wq_sem.at[g, third],
            )
            load.start()
            wq_loads.append(load)
    load_out = pltpu.make_async_copy(wo_hbm, wo, wo_sem)
    load_out.start()

    def send_all(src, dst, send, recv, a, b):
        for to in peers:
            pltpu.make_async_remote_copy(
                src_ref=src.at[to, :, pl.ds(a, b - a)],
                dst_ref=dst.at[me, :, pl.ds(a, b - a)],
                send_sem=send,
                recv_sem=recv,
                device_id={"frame": to},
                device_id_type=MESH,
            ).start()

    def all_copies(src, dst, send, recv, a, b):
        return pltpu.make_async_remote_copy(
            src_ref=src.at[pl.ds(0, n - 1), :, pl.ds(a, b - a)],
            dst_ref=dst.at[pl.ds(0, n - 1), :, pl.ds(a, b - a)],
            send_sem=send,
            recv_sem=recv,
            device_id={"frame": peers[0]},
            device_id_type=MESH,
        )

    gains[0].wait()
    for c in range(CHUNKS):
        lat_loads[c].wait()
        block = lat[c * half_rows : (c + 1) * half_rows]
        values = block.astype(F32).reshape(tokens, model)
        center = values - jnp.mean(values, axis=-1, keepdims=True)
        spread = jnp.mean(center * center, axis=-1, keepdims=True)
        normed = center * lax.rsqrt(spread + 1e-06) * ln_ref[...].reshape(1, model)
        xs[c] = normed.reshape(n, places, model).astype(BF16)
        if c == 0:
            pl.semaphore_wait(barrier, n - 1)
        send_all(xs.at[c], xr.at[c], s1.at[c], r1.at[c], 0, model)
    for c in range(CHUNKS):
        xr[c, pl.ds(me, 1)] = xs[c, pl.ds(me, 1)]

    gains[1].wait()
    gains[2].wait()
    entry = lax.broadcasted_iota(jnp.int32, (HEAD_DIM, model), 0)
    place = lax.broadcasted_iota(jnp.int32, (HEAD_DIM, model), 1)
    repeat = (lax.rem(place, HEAD_DIM) == entry).astype(F32)
    both = qg_ref[...] * kg_ref[...] * (HEAD_DIM**-0.5 * LOG2_E)
    gain = jnp.dot(
        jnp.broadcast_to(both.reshape(1, HEAD_DIM), (8, HEAD_DIM)),
        repeat,
        preferred_element_type=F32,
        precision=lax.Precision.HIGHEST,
    )[0:1]

    def head_of(shape, axis, p):
        lane = lax.broadcasted_iota(jnp.int32, shape, axis) + (p * LANES - 2 * p * HEAD_DIM)
        return jnp.where(lane < 0, -1, jnp.where(lane < HEAD_DIM, 0, jnp.where(lane < 2 * HEAD_DIM, 1, 2)))

    def one_zero(mask):
        return jnp.where(mask, 1.0, 0.0).astype(BF16)

    for p in range(pairs):
        down = head_of((WINDOW, 1), 0, p)
        over = head_of((1, WINDOW), 1, p)
        key_sum[p] = one_zero(down == over)
        slot = lax.div(lax.broadcasted_iota(jnp.int32, (1, 2 * tokens), 1), tokens)
        query_sum[p] = one_zero(down == slot)
        slot = lax.div(lax.broadcasted_iota(jnp.int32, (2 * tokens, 1), 0), tokens)
        ones[p] = one_zero(slot == over)
    row_i = lax.broadcasted_iota(jnp.int32, (tokens, 2 * tokens), 0)
    col_i = lax.broadcasted_iota(jnp.int32, (tokens, 2 * tokens), 1)
    same = lax.rem(row_i, places) == lax.rem(col_i, places)

    for c in range(CHUNKS):
        carry = None
        for g in range(groups):
            a, b = MID_CUTS[g], MID_CUTS[g + 1]
            if c == 0:
                for load in wq_loads[3 * g : 3 * g + 3]:
                    load.wait()
            if g == 0:
                all_copies(xs.at[c], xr.at[c], s1.at[c], r1.at[c], 0, model).wait_recv()
                part = xr[c].astype(F32).reshape(tokens, model).astype(BF16)
            weights = wq_parts[g]
            width = b - a
            for col in range(0, 3 * width, STEP):
                end = min(col + STEP, 3 * width)
                product = jnp.dot(part, weights[:, col:end], preferred_element_type=F32)
                for tile in range(col, end, LANES):
                    to = tile // width * model + a + tile % width
                    acc[:, to : to + LANES] = product[:, tile - col : tile - col + LANES]

            for p in range(PAIR_CUTS[g], PAIR_CUTS[g + 1]):
                lo, hi = p * LANES, p * LANES + WINDOW
                over = head_of((1, WINDOW), 1, p)
                query = acc[:, lo:hi]
                keys = acc[:, model + lo : model + hi]
                vals = acc[:, 2 * model + lo : 2 * model + hi]
                k_sum = jnp.dot((keys * keys).astype(BF16), key_sum[p], preferred_element_type=F32)
                q_sum = jnp.dot((query * query).astype(BF16), query_sum[p], preferred_element_type=F32)
                keys = keys * lax.rsqrt(k_sum * (1.0 / HEAD_DIM) + 1e-06) * gain[:, lo:hi]
                keys = jnp.concatenate(
                    [jnp.where(over == 0, keys, 0.0), jnp.where(over == 1, keys, 0.0)], axis=0
                ).astype(BF16)
                vals = jnp.concatenate(
                    [jnp.where(over == 0, vals, 0.0), jnp.where(over == 1, vals, 0.0)], axis=0
                ).astype(BF16)
                scores = lax.dot_general(
                    query.astype(BF16), keys, (((1,), (1,)), ((), ())), preferred_element_type=F32
                )
                scores = scores * lax.rsqrt(q_sum * (1.0 / HEAD_DIM) + 1e-06)
                probs = jnp.where(same, jnp.exp2(scores), 0.0).astype(BF16)
                top = jnp.dot(probs, vals, preferred_element_type=F32)
                total = jnp.dot(probs, ones[p], preferred_element_type=F32)
                first_top, first_total = top[:, :LANES], total[:, :LANES]
                if carry is not None:
                    first_top = first_top + carry[0]
                    first_total = first_total + carry[1]
                done = first_top / first_total
                ys[c, :, :, lo : lo + LANES] = done.reshape(n, places, LANES).astype(BF16)
                carry = (top[:, LANES:], total[:, LANES:])
            if g == groups - 1:
                done = carry[0] / carry[1]
                ys[c, :, :, model - LANES :] = done.reshape(n, places, LANES).astype(BF16)
            a, b = OUT_CUTS[g], OUT_CUTS[g + 1]
            send_all(ys.at[c], yr.at[c], s2.at[c, g], r2.at[c, g], a, b)
        yr[c, pl.ds(me, 1)] = ys[c, pl.ds(me, 1)]

    load_out.wait()
    for c in range(CHUNKS):
        all_copies(xs.at[c], xr.at[c], s1.at[c], r1.at[c], 0, model).wait_send()
    for c in range(CHUNKS):
        piece = pl.ds(c * half_rows, half_rows)
        branch = lat[c * half_rows : (c + 1) * half_rows].astype(F32).reshape(tokens, model)
        for g in range(groups):
            a, b = OUT_CUTS[g], OUT_CUTS[g + 1]
            all_copies(ys.at[c], yr.at[c], s2.at[c, g], r2.at[c, g], a, b).wait_recv()
            part = yr[c, :, :, a:b].astype(F32).reshape(tokens, b - a).astype(BF16)
            product = jnp.dot(part, wo[a:b, :], preferred_element_type=F32)
            if g == 0:
                acc[:, :model] = product
            else:
                branch = branch + (acc[:, :model] + product)
                out_ref[piece] = branch.reshape(half_rows, columns, model).astype(BF16)
    for c in range(CHUNKS):
        for g in range(groups):
            a, b = OUT_CUTS[g], OUT_CUTS[g + 1]
            all_copies(ys.at[c], yr.at[c], s2.at[c, g], r2.at[c, g], a, b).wait_send()


def fused(n, latent, ln_gain, q_gain, k_gain, w_qkv, w_out):
    rows, columns, model = latent.shape
    places = rows * columns // (n * CHUNKS)
    tokens = n * places
    vmem = pl.BlockSpec(memory_space=pltpu.VMEM)
    hbm = pl.BlockSpec(memory_space=pltpu.HBM)
    block = pltpu.VMEM((CHUNKS, n, places, model), BF16)
    groups = len(MID_CUTS) - 1
    pairs = HEADS // 2
    dma = pltpu.SemaphoreType.DMA
    return pl.pallas_call(
        functools.partial(kernel, n),
        out_shape=jax.ShapeDtypeStruct(latent.shape, BF16),
        in_specs=[hbm] * 6,
        out_specs=vmem,
        scratch_shapes=[
            pltpu.VMEM(latent.shape, BF16),
            pltpu.VMEM(ln_gain.shape, F32),
            pltpu.VMEM(q_gain.shape, F32),
            pltpu.VMEM(k_gain.shape, F32),
            block,
            block,
            block,
            block,
            pltpu.VMEM((model, 3 * (MID_CUTS[1] - MID_CUTS[0])), BF16),
            pltpu.VMEM((model, 3 * (MID_CUTS[2] - MID_CUTS[1])), BF16),
            pltpu.VMEM(w_out.shape, BF16),
            pltpu.VMEM((tokens, w_qkv.shape[1]), F32),
            pltpu.VMEM((pairs, WINDOW, WINDOW), BF16),
            pltpu.VMEM((pairs, WINDOW, 2 * tokens), BF16),
            pltpu.VMEM((pairs, 2 * tokens, WINDOW), BF16),
            dma((CHUNKS,)),
            dma((3,)),
            dma((groups, 3)),
            dma,
            dma((CHUNKS,)),
            dma((CHUNKS,)),
            dma((CHUNKS, groups)),
            dma((CHUNKS, groups)),
        ],
        compiler_params=pltpu.CompilerParams(
            collective_id=0, has_side_effects=True, vmem_limit_bytes=VMEM_BYTES
        ),
    )(
        *(
            pltpu.with_memory_space_constraint(value, pltpu.HBM)
            for value in (latent, ln_gain, q_gain, k_gain, w_qkv, w_out)
        )
    )


def layer_norm(rows, ln_gain):
    values = rows.astype(jnp.float32)
    center = values - jnp.mean(values, axis=-1, keepdims=True)
    spread = jnp.mean(center * center, axis=-1, keepdims=True)
    return (center * lax.rsqrt(spread + 1e-06) * ln_gain).astype(jnp.bfloat16)


def head_norm(values, gain):
    shaped = values.reshape(values.shape[:-1] + (HEADS, HEAD_DIM))
    mean_sq = jnp.mean(shaped * shaped, axis=-1, keepdims=True)
    return (shaped * lax.rsqrt(mean_sq + 1e-06) * gain).astype(jnp.bfloat16).reshape(values.shape)


def project(normed, w_qkv, q_gain, k_gain):
    width = normed.shape[-1]
    mixed = jnp.dot(normed.reshape(-1, width), w_qkv, preferred_element_type=jnp.float32)
    mixed = mixed.reshape(normed.shape[:-1] + (3 * width,))
    query = head_norm(mixed[..., :width], q_gain)
    keys = head_norm(mixed[..., width : 2 * width], k_gain)
    values = mixed[..., 2 * width :].astype(jnp.bfloat16)
    return (query, keys, values)


def attend(query, keys, values):
    lead = query.shape[0]
    others = query.shape[1]
    q_four = query.reshape(lead, others, HEADS, HEAD_DIM)
    k_four = keys.reshape(lead, others, HEADS, HEAD_DIM)
    v_four = values.reshape(lead, others, HEADS, HEAD_DIM)
    scores = jnp.einsum(
        "tshe,ushe->shtu", q_four, k_four, preferred_element_type=jnp.float32
    ) * HEAD_DIM ** (-0.5)
    weights = jnp.exp(scores)
    weights = (weights / jnp.sum(weights, axis=-1, keepdims=True)).astype(jnp.bfloat16)
    mixed = jnp.einsum("shtu,ushe->tshe", weights, v_four, preferred_element_type=jnp.float32)
    return mixed.astype(jnp.bfloat16).reshape(query.shape)


def body(latent, ln_gain, q_gain, k_gain, w_qkv, w_out):
    device_count = lax.axis_size("frame")
    rows, columns, model = latent.shape
    positions = rows * columns
    per_peer = positions // device_count
    if per_peer % 8 == 0 and rows % CHUNKS == 0 and device_count % 2 == 0:
        return fused(device_count, latent, ln_gain, q_gain, k_gain, w_qkv, w_out)
    flat = latent.reshape(positions, model)
    normed = layer_norm(flat, ln_gain)
    query, keys, values = project(
        lax.all_to_all(
            normed.reshape(device_count, per_peer, model),
            "frame",
            split_axis=0,
            concat_axis=0,
            tiled=True,
        ),
        w_qkv,
        q_gain,
        k_gain,
    )
    mixed = attend(query, keys, values)
    returned = lax.all_to_all(mixed, "frame", split_axis=0, concat_axis=0, tiled=True)
    attended = returned.reshape(positions, model)
    branch = jnp.dot(attended, w_out, preferred_element_type=jnp.float32)
    result = flat.astype(jnp.float32) + branch
    return result.astype(jnp.bfloat16).reshape(latent.shape)


def solution(mesh):
    placed = (P(("groups", "frame"), None, None), P(), P(), P(), P(), P())
    return jax.shard_map(
        body,
        mesh=mesh,
        in_specs=placed,
        out_specs=P(("groups", "frame"), None, None),
        check_vma=False,
    )
```

```python
import functools

import jax
import jax.numpy as jnp
from jax import lax
from jax.experimental import pallas as pl
from jax.experimental.pallas import tpu as pltpu
from jax.sharding import PartitionSpec as P

HEADS = 16
HEAD_DIM = 72
LANES = 128
WINDOW = 256
CHUNKS = 2
MID_CUTS = (0, 640, 1152)
OUT_CUTS = (0, 512, 1152)
PAIR_CUTS = (0, 4, 8)
STEP = 256
VMEM_BYTES = 30000000
MESH = pl.DeviceIdType.MESH
F32 = jnp.float32
BF16 = jnp.bfloat16
LOG2_E = 1.4426950408889634


def kernel(
    n,
    lat_hbm,
    ln_hbm,
    qg_hbm,
    kg_hbm,
    wq_hbm,
    wo_hbm,
    out_ref,
    lat,
    ln_ref,
    qg_ref,
    kg_ref,
    xs,
    xr,
    ys,
    yr,
    wq0,
    wq1,
    wo,
    acc,
    key_sum,
    query_sum,
    ones,
    lat_sem,
    gain_sem,
    wq_sem,
    wo_sem,
    s1,
    r1,
    s2,
    r2,
):
    rows, columns, model = lat_hbm.shape
    places = rows * columns // (n * CHUNKS)
    tokens = n * places
    half_rows = rows // CHUNKS
    groups = len(MID_CUTS) - 1
    pairs = HEADS // 2
    me = lax.axis_index("frame")
    peers = [lax.rem(me + k, n) for k in range(1, n)]
    ascending = [k + (me <= k).astype(jnp.int32) for k in range(n - 1)]

    barrier = pltpu.get_barrier_semaphore()
    for to in peers:
        pl.semaphore_signal(barrier, inc=1, device_id={"frame": to}, device_id_type=MESH)

    lat_loads = []
    for c in range(CHUNKS):
        part = pl.ds(c * half_rows, half_rows)
        lat_loads.append(pltpu.make_async_copy(lat_hbm.at[part], lat.at[part], lat_sem.at[c]))
        lat_loads[-1].start()
    gains = [
        pltpu.make_async_copy(src, dst, gain_sem.at[i])
        for i, (src, dst) in enumerate(((ln_hbm, ln_ref), (qg_hbm, qg_ref), (kg_hbm, kg_ref)))
    ]
    for load in gains:
        load.start()
    wq_parts = (wq0, wq1)
    wq_loads = []
    for g in range(groups):
        a, b = MID_CUTS[g], MID_CUTS[g + 1]
        for third in range(3):
            load = pltpu.make_async_copy(
                wq_hbm.at[:, pl.ds(third * model + a, b - a)],
                wq_parts[g].at[:, pl.ds(third * (b - a), b - a)],
                wq_sem.at[g, third],
            )
            wq_loads.append(load)
    load_out = pltpu.make_async_copy(wo_hbm, wo, wo_sem)

    def send_all(src, dst, send, recv, a, b, order):
        for to in order:
            pltpu.make_async_remote_copy(
                src_ref=src.at[to, :, pl.ds(a, b - a)],
                dst_ref=dst.at[me, :, pl.ds(a, b - a)],
                send_sem=send,
                recv_sem=recv,
                device_id={"frame": to},
                device_id_type=MESH,
            ).start()

    def all_copies(src, dst, send, recv, a, b):
        return pltpu.make_async_remote_copy(
            src_ref=src.at[pl.ds(0, n - 1), :, pl.ds(a, b - a)],
            dst_ref=dst.at[pl.ds(0, n - 1), :, pl.ds(a, b - a)],
            send_sem=send,
            recv_sem=recv,
            device_id={"frame": peers[0]},
            device_id_type=MESH,
        )

    gains[0].wait()
    for c in range(CHUNKS):
        lat_loads[c].wait()
        block = lat[c * half_rows : (c + 1) * half_rows]
        values = block.astype(F32).reshape(tokens, model)
        center = values - jnp.mean(values, axis=-1, keepdims=True)
        spread = jnp.mean(center * center, axis=-1, keepdims=True)
        normed = center * lax.rsqrt(spread + 1e-06) * ln_ref[...].reshape(1, model)
        xs[c] = normed.reshape(n, places, model).astype(BF16)
        if c == 0:
            pl.semaphore_wait(barrier, n - 1)
        send_all(xs.at[c], xr.at[c], s1.at[c], r1.at[c], 0, model, peers)
    for load in wq_loads:
        load.start()
    load_out.start()
    for c in range(CHUNKS):
        xr[c, pl.ds(me, 1)] = xs[c, pl.ds(me, 1)]

    gains[1].wait()
    gains[2].wait()
    entry = lax.broadcasted_iota(jnp.int32, (HEAD_DIM, model), 0)
    place = lax.broadcasted_iota(jnp.int32, (HEAD_DIM, model), 1)
    repeat = (lax.rem(place, HEAD_DIM) == entry).astype(F32)
    both = qg_ref[...] * kg_ref[...] * (HEAD_DIM**-0.5 * LOG2_E)
    gain = jnp.dot(
        jnp.broadcast_to(both.reshape(1, HEAD_DIM), (8, HEAD_DIM)),
        repeat,
        preferred_element_type=F32,
        precision=lax.Precision.HIGHEST,
    )[0:1]

    def head_of(shape, axis, p):
        lane = lax.broadcasted_iota(jnp.int32, shape, axis) + (p * LANES - 2 * p * HEAD_DIM)
        return jnp.where(lane < 0, -1, jnp.where(lane < HEAD_DIM, 0, jnp.where(lane < 2 * HEAD_DIM, 1, 2)))

    def one_zero(mask):
        return jnp.where(mask, 1.0, 0.0).astype(BF16)

    for p in range(pairs):
        down = head_of((WINDOW, 1), 0, p)
        over = head_of((1, WINDOW), 1, p)
        key_sum[p] = one_zero(down == over)
        slot = lax.div(lax.broadcasted_iota(jnp.int32, (1, 2 * tokens), 1), tokens)
        query_sum[p] = one_zero(down == slot)
        slot = lax.div(lax.broadcasted_iota(jnp.int32, (2 * tokens, 1), 0), tokens)
        ones[p] = one_zero(slot == over)
    row_i = lax.broadcasted_iota(jnp.int32, (tokens, 2 * tokens), 0)
    col_i = lax.broadcasted_iota(jnp.int32, (tokens, 2 * tokens), 1)
    same = lax.rem(row_i, places) == lax.rem(col_i, places)

    for c in range(CHUNKS):
        carry = None
        for g in range(groups):
            a, b = MID_CUTS[g], MID_CUTS[g + 1]
            if c == 0:
                for load in wq_loads[3 * g : 3 * g + 3]:
                    load.wait()
            if g == 0:
                all_copies(xs.at[c], xr.at[c], s1.at[c], r1.at[c], 0, model).wait_recv()
                part = xr[c].astype(F32).reshape(tokens, model).astype(BF16)
            weights = wq_parts[g]
            width = b - a
            for col in range(0, 3 * width, STEP):
                end = min(col + STEP, 3 * width)
                product = jnp.dot(part, weights[:, col:end], preferred_element_type=F32)
                for tile in range(col, end, LANES):
                    to = tile // width * model + a + tile % width
                    acc[:, to : to + LANES] = product[:, tile - col : tile - col + LANES]

            span = range(PAIR_CUTS[g], PAIR_CUTS[g + 1])
            k_sums, q_sums, scores, probs, tops, totals = {}, {}, {}, {}, {}, {}
            for p in span:
                lo, hi = p * LANES, p * LANES + WINDOW
                query = acc[:, lo:hi]
                keys = acc[:, model + lo : model + hi]
                k_sums[p] = jnp.dot((keys * keys).astype(BF16), key_sum[p], preferred_element_type=F32)
                q_sums[p] = jnp.dot(
                    (query * query).astype(BF16), query_sum[p], preferred_element_type=F32
                )
            for p in span:
                lo, hi = p * LANES, p * LANES + WINDOW
                over = head_of((1, WINDOW), 1, p)
                keys = acc[:, model + lo : model + hi]
                keys = keys * lax.rsqrt(k_sums[p] * (1.0 / HEAD_DIM) + 1e-06) * gain[:, lo:hi]
                keys = jnp.concatenate(
                    [jnp.where(over == 0, keys, 0.0), jnp.where(over == 1, keys, 0.0)], axis=0
                ).astype(BF16)
                scores[p] = lax.dot_general(
                    acc[:, lo:hi].astype(BF16),
                    keys,
                    (((1,), (1,)), ((), ())),
                    preferred_element_type=F32,
                )
            for p in span:
                scaled = scores[p] * lax.rsqrt(q_sums[p] * (1.0 / HEAD_DIM) + 1e-06)
                probs[p] = jnp.where(same, jnp.exp2(scaled), 0.0).astype(BF16)
            for p in span:
                lo, hi = p * LANES, p * LANES + WINDOW
                over = head_of((1, WINDOW), 1, p)
                vals = acc[:, 2 * model + lo : 2 * model + hi]
                vals = jnp.concatenate(
                    [jnp.where(over == 0, vals, 0.0), jnp.where(over == 1, vals, 0.0)], axis=0
                ).astype(BF16)
                tops[p] = jnp.dot(probs[p], vals, preferred_element_type=F32)
                totals[p] = jnp.dot(probs[p], ones[p], preferred_element_type=F32)
            for p in span:
                lo = p * LANES
                top, total = tops[p][:, :LANES], totals[p][:, :LANES]
                if carry is not None:
                    top, total = top + carry[0], total + carry[1]
                ys[c, :, :, lo : lo + LANES] = (top / total).reshape(n, places, LANES).astype(BF16)
                carry = (tops[p][:, LANES:], totals[p][:, LANES:])
            if g == groups - 1:
                done = carry[0] / carry[1]
                ys[c, :, :, model - LANES :] = done.reshape(n, places, LANES).astype(BF16)
            a, b = OUT_CUTS[g], OUT_CUTS[g + 1]
            send_all(ys.at[c], yr.at[c], s2.at[c, g], r2.at[c, g], a, b, ascending)
        yr[c, pl.ds(me, 1)] = ys[c, pl.ds(me, 1)]

    load_out.wait()
    for c in range(CHUNKS):
        all_copies(xs.at[c], xr.at[c], s1.at[c], r1.at[c], 0, model).wait_send()
    for c in range(CHUNKS):
        piece = pl.ds(c * half_rows, half_rows)
        branch = lat[c * half_rows : (c + 1) * half_rows].astype(F32).reshape(tokens, model)
        for g in range(groups):
            a, b = OUT_CUTS[g], OUT_CUTS[g + 1]
            all_copies(ys.at[c], yr.at[c], s2.at[c, g], r2.at[c, g], a, b).wait_recv()
            part = yr[c, :, :, a:b].astype(F32).reshape(tokens, b - a).astype(BF16)
            product = jnp.dot(part, wo[a:b, :], preferred_element_type=F32)
            if g == 0:
                acc[:, :model] = product
            else:
                branch = branch + (acc[:, :model] + product)
                out_ref[piece] = branch.reshape(half_rows, columns, model).astype(BF16)
    for c in range(CHUNKS):
        for g in range(groups):
            a, b = OUT_CUTS[g], OUT_CUTS[g + 1]
            all_copies(ys.at[c], yr.at[c], s2.at[c, g], r2.at[c, g], a, b).wait_send()


def fused(n, latent, ln_gain, q_gain, k_gain, w_qkv, w_out):
    rows, columns, model = latent.shape
    places = rows * columns // (n * CHUNKS)
    tokens = n * places
    vmem = pl.BlockSpec(memory_space=pltpu.VMEM)
    hbm = pl.BlockSpec(memory_space=pltpu.HBM)
    block = pltpu.VMEM((CHUNKS, n, places, model), BF16)
    groups = len(MID_CUTS) - 1
    pairs = HEADS // 2
    dma = pltpu.SemaphoreType.DMA
    return pl.pallas_call(
        functools.partial(kernel, n),
        out_shape=jax.ShapeDtypeStruct(latent.shape, BF16),
        in_specs=[hbm] * 6,
        out_specs=vmem,
        scratch_shapes=[
            pltpu.VMEM(latent.shape, BF16),
            pltpu.VMEM(ln_gain.shape, F32),
            pltpu.VMEM(q_gain.shape, F32),
            pltpu.VMEM(k_gain.shape, F32),
            block,
            block,
            block,
            block,
            pltpu.VMEM((model, 3 * (MID_CUTS[1] - MID_CUTS[0])), BF16),
            pltpu.VMEM((model, 3 * (MID_CUTS[2] - MID_CUTS[1])), BF16),
            pltpu.VMEM(w_out.shape, BF16),
            pltpu.VMEM((tokens, w_qkv.shape[1]), F32),
            pltpu.VMEM((pairs, WINDOW, WINDOW), BF16),
            pltpu.VMEM((pairs, WINDOW, 2 * tokens), BF16),
            pltpu.VMEM((pairs, 2 * tokens, WINDOW), BF16),
            dma((CHUNKS,)),
            dma((3,)),
            dma((groups, 3)),
            dma,
            dma((CHUNKS,)),
            dma((CHUNKS,)),
            dma((CHUNKS, groups)),
            dma((CHUNKS, groups)),
        ],
        compiler_params=pltpu.CompilerParams(
            collective_id=0, has_side_effects=True, vmem_limit_bytes=VMEM_BYTES
        ),
    )(
        *(
            pltpu.with_memory_space_constraint(value, pltpu.HBM)
            for value in (latent, ln_gain, q_gain, k_gain, w_qkv, w_out)
        )
    )


def layer_norm(rows, ln_gain):
    values = rows.astype(jnp.float32)
    center = values - jnp.mean(values, axis=-1, keepdims=True)
    spread = jnp.mean(center * center, axis=-1, keepdims=True)
    return (center * lax.rsqrt(spread + 1e-06) * ln_gain).astype(jnp.bfloat16)


def head_norm(values, gain):
    shaped = values.reshape(values.shape[:-1] + (HEADS, HEAD_DIM))
    mean_sq = jnp.mean(shaped * shaped, axis=-1, keepdims=True)
    return (shaped * lax.rsqrt(mean_sq + 1e-06) * gain).astype(jnp.bfloat16).reshape(values.shape)


def project(normed, w_qkv, q_gain, k_gain):
    width = normed.shape[-1]
    mixed = jnp.dot(normed.reshape(-1, width), w_qkv, preferred_element_type=jnp.float32)
    mixed = mixed.reshape(normed.shape[:-1] + (3 * width,))
    query = head_norm(mixed[..., :width], q_gain)
    keys = head_norm(mixed[..., width : 2 * width], k_gain)
    values = mixed[..., 2 * width :].astype(jnp.bfloat16)
    return (query, keys, values)


def attend(query, keys, values):
    lead = query.shape[0]
    others = query.shape[1]
    q_four = query.reshape(lead, others, HEADS, HEAD_DIM)
    k_four = keys.reshape(lead, others, HEADS, HEAD_DIM)
    v_four = values.reshape(lead, others, HEADS, HEAD_DIM)
    scores = jnp.einsum(
        "tshe,ushe->shtu", q_four, k_four, preferred_element_type=jnp.float32
    ) * HEAD_DIM ** (-0.5)
    weights = jnp.exp(scores)
    weights = (weights / jnp.sum(weights, axis=-1, keepdims=True)).astype(jnp.bfloat16)
    mixed = jnp.einsum("shtu,ushe->tshe", weights, v_four, preferred_element_type=jnp.float32)
    return mixed.astype(jnp.bfloat16).reshape(query.shape)


def body(latent, ln_gain, q_gain, k_gain, w_qkv, w_out):
    device_count = lax.axis_size("frame")
    rows, columns, model = latent.shape
    positions = rows * columns
    per_peer = positions // device_count
    if per_peer % 8 == 0 and rows % CHUNKS == 0 and device_count % 2 == 0:
        return fused(device_count, latent, ln_gain, q_gain, k_gain, w_qkv, w_out)
    flat = latent.reshape(positions, model)
    normed = layer_norm(flat, ln_gain)
    query, keys, values = project(
        lax.all_to_all(
            normed.reshape(device_count, per_peer, model),
            "frame",
            split_axis=0,
            concat_axis=0,
            tiled=True,
        ),
        w_qkv,
        q_gain,
        k_gain,
    )
    mixed = attend(query, keys, values)
    returned = lax.all_to_all(mixed, "frame", split_axis=0, concat_axis=0, tiled=True)
    attended = returned.reshape(positions, model)
    branch = jnp.dot(attended, w_out, preferred_element_type=jnp.float32)
    result = flat.astype(jnp.float32) + branch
    return result.astype(jnp.bfloat16).reshape(latent.shape)


def solution(mesh):
    placed = (P(("groups", "frame"), None, None), P(), P(), P(), P(), P())
    return jax.shard_map(
        body,
        mesh=mesh,
        in_specs=placed,
        out_specs=P(("groups", "frame"), None, None),
        check_vma=False,
    )
```

```python
import functools

import jax
import jax.numpy as jnp
from jax import lax
from jax.experimental import pallas as pl
from jax.experimental.pallas import tpu as pltpu
from jax.sharding import PartitionSpec as P

HEADS = 16
HEAD_DIM = 72
LANES = 128
WINDOW = 256
CHUNKS = 2
MID_CUTS = (0, 1152)
OUT_CUTS = (0, 1152)
PAIR_CUTS = (0, 8)
PLANE = 4
STEP = 256
VMEM_BYTES = 30000000
MESH = pl.DeviceIdType.MESH
F32 = jnp.float32
BF16 = jnp.bfloat16
LOG2_E = 1.4426950408889634


def kernel(
    n,
    lat_hbm,
    ln_hbm,
    qg_hbm,
    kg_hbm,
    wq_hbm,
    wo_hbm,
    out_ref,
    lat,
    ln_ref,
    qg_ref,
    kg_ref,
    xs,
    xr,
    ys,
    yr,
    wq0,
    wo,
    acc,
    key_sum,
    query_sum,
    ones,
    lat_sem,
    gain_sem,
    wq_sem,
    wo_sem,
    s1,
    r1,
    s2,
    r2,
    ready,
):
    rows, columns, model = lat_hbm.shape
    places = rows * columns // (n * CHUNKS)
    tokens = n * places
    half_rows = rows // CHUNKS
    groups = len(MID_CUTS) - 1
    pairs = HEADS // 2
    me = lax.axis_index("frame")
    planes = n // PLANE
    depth = lax.div(me, PLANE)
    spot = lax.rem(me, PLANE)
    turn = [lax.rem(spot + k, PLANE) for k in range(PLANE)]
    ascending = [k + (me <= k).astype(jnp.int32) for k in range(n - 1)]

    def tell(semaphore, to):
        pl.semaphore_signal(semaphore, inc=1, device_id={"frame": to}, device_id_type=MESH)

    lat_loads = []
    for c in range(CHUNKS):
        part = pl.ds(c * half_rows, half_rows)
        lat_loads.append(pltpu.make_async_copy(lat_hbm.at[part], lat.at[part], lat_sem.at[c]))
    gains = [
        pltpu.make_async_copy(src, dst, gain_sem.at[i])
        for i, (src, dst) in enumerate(((ln_hbm, ln_ref), (qg_hbm, qg_ref), (kg_hbm, kg_ref)))
    ]
    for load in (lat_loads[0], gains[0], lat_loads[1], gains[1], gains[2]):
        load.start()

    for plane in range(planes - 1, 0, -1):

        @pl.when(depth < plane)
        def _():
            for t in turn:
                tell(pltpu.get_barrier_semaphore(), plane * PLANE + t)

    for k in range(1, PLANE):

        @pl.when(spot + k < PLANE)
        def _():
            tell(pltpu.get_barrier_semaphore(), me + k)

    wq_parts = (wq0,)
    wq_loads = []
    for g in range(groups):
        a, b = MID_CUTS[g], MID_CUTS[g + 1]
        for third in range(3):
            load = pltpu.make_async_copy(
                wq_hbm.at[:, pl.ds(third * model + a, b - a)],
                wq_parts[g].at[:, pl.ds(third * (b - a), b - a)],
                wq_sem.at[g, third],
            )
            wq_loads.append(load)
    load_out = pltpu.make_async_copy(wo_hbm, wo, wo_sem)

    def send_all(src, dst, send, recv, a, b, order):
        for to in order:
            pltpu.make_async_remote_copy(
                src_ref=src.at[to, :, pl.ds(a, b - a)],
                dst_ref=dst.at[me, :, pl.ds(a, b - a)],
                send_sem=send,
                recv_sem=recv,
                device_id={"frame": to},
                device_id_type=MESH,
            ).start()

    def all_copies(src, dst, send, recv, a, b):
        return pltpu.make_async_remote_copy(
            src_ref=src.at[pl.ds(0, n - 1), :, pl.ds(a, b - a)],
            dst_ref=dst.at[pl.ds(0, n - 1), :, pl.ds(a, b - a)],
            send_sem=send,
            recv_sem=recv,
            device_id={"frame": ascending[0]},
            device_id_type=MESH,
        )

    def normalize(c):
        lat_loads[c].wait()
        block = lat[c * half_rows : (c + 1) * half_rows]
        values = block.astype(F32).reshape(tokens, model)
        center = values - jnp.mean(values, axis=-1, keepdims=True)
        spread = jnp.mean(center * center, axis=-1, keepdims=True)
        normed = center * lax.rsqrt(spread + 1e-06) * ln_ref[...].reshape(1, model)
        xs[c] = normed.reshape(n, places, model).astype(BF16)

    def send_normed(c, order):
        send_all(xs.at[c], xr.at[c], s1.at[c], r1.at[c], 0, model, order)

    @pl.when(me > 0)
    def _():
        pl.semaphore_wait(pltpu.get_barrier_semaphore(), me)

    for plane in range(planes - 1):

        @pl.when(plane < depth)
        def _():
            for t in turn:
                tell(ready.at[depth], plane * PLANE + t)

    for k in range(1, PLANE):

        @pl.when(spot >= k)
        def _():
            tell(ready.at[depth], me - k)

    gains[0].wait()
    normalize(0)
    for plane in range(planes):
        if plane == planes - 1:
            normalize(1)
        missing = jnp.where(plane > depth, PLANE, jnp.where(plane == depth, PLANE - 1 - spot, 0))

        @pl.when(missing > 0)
        def _():
            pl.semaphore_wait(ready.at[plane], missing)

        @pl.when(plane != depth)
        def _():
            send_normed(0, [plane * PLANE + turn[0]])

        send_normed(0, [plane * PLANE + t for t in turn[1:]])
    send_normed(1, ascending)
    for load in wq_loads:
        load.start()
    load_out.start()
    for c in range(CHUNKS):
        xr[c, pl.ds(me, 1)] = xs[c, pl.ds(me, 1)]

    gains[1].wait()
    gains[2].wait()
    entry = lax.broadcasted_iota(jnp.int32, (HEAD_DIM, model), 0)
    place = lax.broadcasted_iota(jnp.int32, (HEAD_DIM, model), 1)
    repeat = (lax.rem(place, HEAD_DIM) == entry).astype(F32)
    both = qg_ref[...] * kg_ref[...] * (HEAD_DIM**-0.5 * LOG2_E)
    gain = jnp.dot(
        jnp.broadcast_to(both.reshape(1, HEAD_DIM), (8, HEAD_DIM)),
        repeat,
        preferred_element_type=F32,
        precision=lax.Precision.HIGHEST,
    )[0:1]

    def head_of(shape, axis, p):
        lane = lax.broadcasted_iota(jnp.int32, shape, axis) + (p * LANES - 2 * p * HEAD_DIM)
        return jnp.where(lane < 0, -1, jnp.where(lane < HEAD_DIM, 0, jnp.where(lane < 2 * HEAD_DIM, 1, 2)))

    def one_zero(mask):
        return jnp.where(mask, 1.0, 0.0).astype(BF16)

    for p in range(pairs):
        down = head_of((WINDOW, 1), 0, p)
        over = head_of((1, WINDOW), 1, p)
        key_sum[p] = one_zero(down == over)
        slot = lax.div(lax.broadcasted_iota(jnp.int32, (1, 2 * tokens), 1), tokens)
        query_sum[p] = one_zero(down == slot)
        slot = lax.div(lax.broadcasted_iota(jnp.int32, (2 * tokens, 1), 0), tokens)
        ones[p] = one_zero(slot == over)
    row_i = lax.broadcasted_iota(jnp.int32, (tokens, 2 * tokens), 0)
    col_i = lax.broadcasted_iota(jnp.int32, (tokens, 2 * tokens), 1)
    same = lax.rem(row_i, places) == lax.rem(col_i, places)

    for c in range(CHUNKS):
        carry = None
        for g in range(groups):
            a, b = MID_CUTS[g], MID_CUTS[g + 1]
            if c == 0:
                for load in wq_loads[3 * g : 3 * g + 3]:
                    load.wait()
            if g == 0:
                all_copies(xs.at[c], xr.at[c], s1.at[c], r1.at[c], 0, model).wait_recv()
                part = xr[c].astype(F32).reshape(tokens, model).astype(BF16)
            weights = wq_parts[g]
            width = b - a
            for col in range(0, 3 * width, STEP):
                end = min(col + STEP, 3 * width)
                product = jnp.dot(part, weights[:, col:end], preferred_element_type=F32)
                for tile in range(col, end, LANES):
                    to = tile // width * model + a + tile % width
                    acc[:, to : to + LANES] = product[:, tile - col : tile - col + LANES]

            span = range(PAIR_CUTS[g], PAIR_CUTS[g + 1])
            k_sums, q_sums, scores, probs, tops, totals = {}, {}, {}, {}, {}, {}
            for p in span:
                lo, hi = p * LANES, p * LANES + WINDOW
                query = acc[:, lo:hi]
                keys = acc[:, model + lo : model + hi]
                k_sums[p] = jnp.dot((keys * keys).astype(BF16), key_sum[p], preferred_element_type=F32)
                q_sums[p] = jnp.dot(
                    (query * query).astype(BF16), query_sum[p], preferred_element_type=F32
                )
            for p in span:
                lo, hi = p * LANES, p * LANES + WINDOW
                over = head_of((1, WINDOW), 1, p)
                keys = acc[:, model + lo : model + hi]
                keys = keys * lax.rsqrt(k_sums[p] * (1.0 / HEAD_DIM) + 1e-06) * gain[:, lo:hi]
                keys = jnp.concatenate(
                    [jnp.where(over == 0, keys, 0.0), jnp.where(over == 1, keys, 0.0)], axis=0
                ).astype(BF16)
                scores[p] = lax.dot_general(
                    acc[:, lo:hi].astype(BF16),
                    keys,
                    (((1,), (1,)), ((), ())),
                    preferred_element_type=F32,
                )
            for p in span:
                scaled = scores[p] * lax.rsqrt(q_sums[p] * (1.0 / HEAD_DIM) + 1e-06)
                probs[p] = jnp.where(same, jnp.exp2(scaled), 0.0).astype(BF16)
            for p in span:
                lo, hi = p * LANES, p * LANES + WINDOW
                over = head_of((1, WINDOW), 1, p)
                vals = acc[:, 2 * model + lo : 2 * model + hi]
                vals = jnp.concatenate(
                    [jnp.where(over == 0, vals, 0.0), jnp.where(over == 1, vals, 0.0)], axis=0
                ).astype(BF16)
                tops[p] = jnp.dot(probs[p], vals, preferred_element_type=F32)
                totals[p] = jnp.dot(probs[p], ones[p], preferred_element_type=F32)
            for p in span:
                lo = p * LANES
                top, total = tops[p][:, :LANES], totals[p][:, :LANES]
                if carry is not None:
                    top, total = top + carry[0], total + carry[1]
                ys[c, :, :, lo : lo + LANES] = (top / total).reshape(n, places, LANES).astype(BF16)
                carry = (tops[p][:, LANES:], totals[p][:, LANES:])
            if g == groups - 1:
                done = carry[0] / carry[1]
                ys[c, :, :, model - LANES :] = done.reshape(n, places, LANES).astype(BF16)
            a, b = OUT_CUTS[g], OUT_CUTS[g + 1]
            send_all(ys.at[c], yr.at[c], s2.at[c, g], r2.at[c, g], a, b, ascending)
        yr[c, pl.ds(me, 1)] = ys[c, pl.ds(me, 1)]

    load_out.wait()
    for c in range(CHUNKS):
        all_copies(xs.at[c], xr.at[c], s1.at[c], r1.at[c], 0, model).wait_send()
    for c in range(CHUNKS):
        piece = pl.ds(c * half_rows, half_rows)
        branch = lat[c * half_rows : (c + 1) * half_rows].astype(F32).reshape(tokens, model)
        for g in range(groups):
            a, b = OUT_CUTS[g], OUT_CUTS[g + 1]
            all_copies(ys.at[c], yr.at[c], s2.at[c, g], r2.at[c, g], a, b).wait_recv()
            part = yr[c, :, :, a:b].astype(F32).reshape(tokens, b - a).astype(BF16)
            product = jnp.dot(part, wo[a:b, :], preferred_element_type=F32)
            out_ref[piece] = (branch + product).reshape(half_rows, columns, model).astype(BF16)
    for c in range(CHUNKS):
        for g in range(groups):
            a, b = OUT_CUTS[g], OUT_CUTS[g + 1]
            all_copies(ys.at[c], yr.at[c], s2.at[c, g], r2.at[c, g], a, b).wait_send()


def fused(n, latent, ln_gain, q_gain, k_gain, w_qkv, w_out):
    rows, columns, model = latent.shape
    places = rows * columns // (n * CHUNKS)
    tokens = n * places
    vmem = pl.BlockSpec(memory_space=pltpu.VMEM)
    hbm = pl.BlockSpec(memory_space=pltpu.HBM)
    block = pltpu.VMEM((CHUNKS, n, places, model), BF16)
    groups = len(MID_CUTS) - 1
    pairs = HEADS // 2
    dma = pltpu.SemaphoreType.DMA
    return pl.pallas_call(
        functools.partial(kernel, n),
        out_shape=jax.ShapeDtypeStruct(latent.shape, BF16),
        in_specs=[hbm] * 6,
        out_specs=vmem,
        scratch_shapes=[
            pltpu.VMEM(latent.shape, BF16),
            pltpu.VMEM(ln_gain.shape, F32),
            pltpu.VMEM(q_gain.shape, F32),
            pltpu.VMEM(k_gain.shape, F32),
            block,
            block,
            block,
            block,
            pltpu.VMEM((model, 3 * (MID_CUTS[1] - MID_CUTS[0])), BF16),
            pltpu.VMEM(w_out.shape, BF16),
            pltpu.VMEM((tokens, w_qkv.shape[1]), F32),
            pltpu.VMEM((pairs, WINDOW, WINDOW), BF16),
            pltpu.VMEM((pairs, WINDOW, 2 * tokens), BF16),
            pltpu.VMEM((pairs, 2 * tokens, WINDOW), BF16),
            dma((CHUNKS,)),
            dma((3,)),
            dma((groups, 3)),
            dma,
            dma((CHUNKS,)),
            dma((CHUNKS,)),
            dma((CHUNKS, groups)),
            dma((CHUNKS, groups)),
            pltpu.SemaphoreType.REGULAR((n // PLANE,)),
        ],
        compiler_params=pltpu.CompilerParams(
            collective_id=0, has_side_effects=True, vmem_limit_bytes=VMEM_BYTES
        ),
    )(
        *(
            pltpu.with_memory_space_constraint(value, pltpu.HBM)
            for value in (latent, ln_gain, q_gain, k_gain, w_qkv, w_out)
        )
    )


def layer_norm(rows, ln_gain):
    values = rows.astype(jnp.float32)
    center = values - jnp.mean(values, axis=-1, keepdims=True)
    spread = jnp.mean(center * center, axis=-1, keepdims=True)
    return (center * lax.rsqrt(spread + 1e-06) * ln_gain).astype(jnp.bfloat16)


def head_norm(values, gain):
    shaped = values.reshape(values.shape[:-1] + (HEADS, HEAD_DIM))
    mean_sq = jnp.mean(shaped * shaped, axis=-1, keepdims=True)
    return (shaped * lax.rsqrt(mean_sq + 1e-06) * gain).astype(jnp.bfloat16).reshape(values.shape)


def project(normed, w_qkv, q_gain, k_gain):
    width = normed.shape[-1]
    mixed = jnp.dot(normed.reshape(-1, width), w_qkv, preferred_element_type=jnp.float32)
    mixed = mixed.reshape(normed.shape[:-1] + (3 * width,))
    query = head_norm(mixed[..., :width], q_gain)
    keys = head_norm(mixed[..., width : 2 * width], k_gain)
    values = mixed[..., 2 * width :].astype(jnp.bfloat16)
    return (query, keys, values)


def attend(query, keys, values):
    lead = query.shape[0]
    others = query.shape[1]
    q_four = query.reshape(lead, others, HEADS, HEAD_DIM)
    k_four = keys.reshape(lead, others, HEADS, HEAD_DIM)
    v_four = values.reshape(lead, others, HEADS, HEAD_DIM)
    scores = jnp.einsum(
        "tshe,ushe->shtu", q_four, k_four, preferred_element_type=jnp.float32
    ) * HEAD_DIM ** (-0.5)
    weights = jnp.exp(scores)
    weights = (weights / jnp.sum(weights, axis=-1, keepdims=True)).astype(jnp.bfloat16)
    mixed = jnp.einsum("shtu,ushe->tshe", weights, v_four, preferred_element_type=jnp.float32)
    return mixed.astype(jnp.bfloat16).reshape(query.shape)


def body(latent, ln_gain, q_gain, k_gain, w_qkv, w_out):
    device_count = lax.axis_size("frame")
    rows, columns, model = latent.shape
    positions = rows * columns
    per_peer = positions // device_count
    if per_peer % 8 == 0 and rows % CHUNKS == 0 and device_count % PLANE == 0:
        return fused(device_count, latent, ln_gain, q_gain, k_gain, w_qkv, w_out)
    flat = latent.reshape(positions, model)
    normed = layer_norm(flat, ln_gain)
    query, keys, values = project(
        lax.all_to_all(
            normed.reshape(device_count, per_peer, model),
            "frame",
            split_axis=0,
            concat_axis=0,
            tiled=True,
        ),
        w_qkv,
        q_gain,
        k_gain,
    )
    mixed = attend(query, keys, values)
    returned = lax.all_to_all(mixed, "frame", split_axis=0, concat_axis=0, tiled=True)
    attended = returned.reshape(positions, model)
    branch = jnp.dot(attended, w_out, preferred_element_type=jnp.float32)
    result = flat.astype(jnp.float32) + branch
    return result.astype(jnp.bfloat16).reshape(latent.shape)


def solution(mesh):
    placed = (P(("groups", "frame"), None, None), P(), P(), P(), P(), P())
    return jax.shard_map(
        body,
        mesh=mesh,
        in_specs=placed,
        out_specs=P(("groups", "frame"), None, None),
        check_vma=False,
    )
```

```python
import functools

import jax
import jax.numpy as jnp
from jax import lax
from jax.experimental import pallas as pl
from jax.experimental.pallas import tpu as pltpu
from jax.sharding import PartitionSpec as P

HEADS = 16
HEAD_DIM = 72
LANES = 128
WINDOW = 256
CHUNKS = 2
MID_CUTS = (0, 1152)
OUT_CUTS = (0, 1152)
PAIR_CUTS = (0, 8)
PLANE = 4
KEY_ROWS = 16
STEP = 256
VMEM_BYTES = 30000000
MESH = pl.DeviceIdType.MESH
F32 = jnp.float32
BF16 = jnp.bfloat16
LOG2_E = 1.4426950408889634


def kernel(
    n,
    lat_hbm,
    ln_hbm,
    qg_hbm,
    kg_hbm,
    wq_hbm,
    wo_hbm,
    out_ref,
    lat,
    ln_ref,
    qg_ref,
    kg_ref,
    xs,
    xr,
    ys,
    yr,
    wq0,
    wo,
    acc,
    key_rows,
    query_sum,
    ones,
    lat_sem,
    gain_sem,
    wq_sem,
    wo_sem,
    s1,
    r1,
    s2,
    r2,
    ready,
):
    rows, columns, model = lat_hbm.shape
    places = rows * columns // (n * CHUNKS)
    tokens = n * places
    half_rows = rows // CHUNKS
    groups = len(MID_CUTS) - 1
    pairs = HEADS // 2
    me = lax.axis_index("frame")
    planes = n // PLANE
    depth = lax.div(me, PLANE)
    spot = lax.rem(me, PLANE)
    turn = [lax.rem(spot + k, PLANE) for k in range(PLANE)]
    ascending = [k + (me <= k).astype(jnp.int32) for k in range(n - 1)]

    def tell(semaphore, to):
        pl.semaphore_signal(semaphore, inc=1, device_id={"frame": to}, device_id_type=MESH)

    lat_loads = []
    for c in range(CHUNKS):
        part = pl.ds(c * half_rows, half_rows)
        lat_loads.append(pltpu.make_async_copy(lat_hbm.at[part], lat.at[part], lat_sem.at[c]))
    gains = [
        pltpu.make_async_copy(src, dst, gain_sem.at[i])
        for i, (src, dst) in enumerate(((ln_hbm, ln_ref), (qg_hbm, qg_ref), (kg_hbm, kg_ref)))
    ]
    for load in (lat_loads[0], gains[0], lat_loads[1], gains[1], gains[2]):
        load.start()

    for plane in range(planes - 1, 0, -1):

        @pl.when(depth < plane)
        def _():
            for t in turn:
                tell(pltpu.get_barrier_semaphore(), plane * PLANE + t)

    for k in range(1, PLANE):

        @pl.when(spot + k < PLANE)
        def _():
            tell(pltpu.get_barrier_semaphore(), me + k)

    wq_parts = (wq0,)
    wq_loads = []
    for g in range(groups):
        a, b = MID_CUTS[g], MID_CUTS[g + 1]
        for third in range(3):
            load = pltpu.make_async_copy(
                wq_hbm.at[:, pl.ds(third * model + a, b - a)],
                wq_parts[g].at[:, pl.ds(third * (b - a), b - a)],
                wq_sem.at[g, third],
            )
            wq_loads.append(load)
    load_out = pltpu.make_async_copy(wo_hbm, wo, wo_sem)

    def send_all(src, dst, send, recv, a, b, order):
        for to in order:
            pltpu.make_async_remote_copy(
                src_ref=src.at[to, :, pl.ds(a, b - a)],
                dst_ref=dst.at[me, :, pl.ds(a, b - a)],
                send_sem=send,
                recv_sem=recv,
                device_id={"frame": to},
                device_id_type=MESH,
            ).start()

    def all_copies(src, dst, send, recv, a, b):
        return pltpu.make_async_remote_copy(
            src_ref=src.at[pl.ds(0, n - 1), :, pl.ds(a, b - a)],
            dst_ref=dst.at[pl.ds(0, n - 1), :, pl.ds(a, b - a)],
            send_sem=send,
            recv_sem=recv,
            device_id={"frame": ascending[0]},
            device_id_type=MESH,
        )

    def normalize(c):
        lat_loads[c].wait()
        block = lat[c * half_rows : (c + 1) * half_rows]
        values = block.astype(F32).reshape(tokens, model)
        center = values - jnp.mean(values, axis=-1, keepdims=True)
        spread = jnp.mean(center * center, axis=-1, keepdims=True)
        normed = center * lax.rsqrt(spread + 1e-06) * ln_ref[...].reshape(1, model)
        xs[c] = normed.reshape(n, places, model).astype(BF16)

    def send_normed(c, order):
        send_all(xs.at[c], xr.at[c], s1.at[c], r1.at[c], 0, model, order)

    @pl.when(me > 0)
    def _():
        pl.semaphore_wait(pltpu.get_barrier_semaphore(), me)

    for plane in range(planes - 1):

        @pl.when(plane < depth)
        def _():
            for t in turn:
                tell(ready.at[depth], plane * PLANE + t)

    for k in range(1, PLANE):

        @pl.when(spot >= k)
        def _():
            tell(ready.at[depth], me - k)

    gains[0].wait()
    normalize(0)
    for plane in range(planes):
        if plane == planes - 1:
            normalize(1)
        missing = jnp.where(plane > depth, PLANE, jnp.where(plane == depth, PLANE - 1 - spot, 0))

        @pl.when(missing > 0)
        def _():
            pl.semaphore_wait(ready.at[plane], missing)

        @pl.when(plane != depth)
        def _():
            send_normed(0, [plane * PLANE + turn[0]])

        send_normed(0, [plane * PLANE + t for t in turn[1:]])
    send_normed(1, ascending)
    for load in wq_loads:
        load.start()
    load_out.start()
    for c in range(CHUNKS):
        xr[c, pl.ds(me, 1)] = xs[c, pl.ds(me, 1)]

    gains[1].wait()
    gains[2].wait()
    entry = lax.broadcasted_iota(jnp.int32, (HEAD_DIM, model), 0)
    place = lax.broadcasted_iota(jnp.int32, (HEAD_DIM, model), 1)
    repeat = (lax.rem(place, HEAD_DIM) == entry).astype(F32)
    both = qg_ref[...] * kg_ref[...] * (HEAD_DIM**-0.5 * LOG2_E)
    gain = jnp.dot(
        jnp.broadcast_to(both.reshape(1, HEAD_DIM), (8, HEAD_DIM)),
        repeat,
        preferred_element_type=F32,
        precision=lax.Precision.HIGHEST,
    )[0:1]

    def head_of(shape, axis, p):
        lane = lax.broadcasted_iota(jnp.int32, shape, axis) + (p * LANES - 2 * p * HEAD_DIM)
        return jnp.where(lane < 0, -1, jnp.where(lane < HEAD_DIM, 0, jnp.where(lane < 2 * HEAD_DIM, 1, 2)))

    def one_zero(mask):
        return jnp.where(mask, 1.0, 0.0).astype(BF16)

    for p in range(pairs):
        down = head_of((WINDOW, 1), 0, p)
        over = head_of((1, WINDOW), 1, p)
        key_rows[p] = one_zero(lax.broadcasted_iota(jnp.int32, (KEY_ROWS, 1), 0) == over)
        slot = lax.div(lax.broadcasted_iota(jnp.int32, (1, 2 * tokens), 1), tokens)
        query_sum[p] = one_zero(down == slot)
        slot = lax.div(lax.broadcasted_iota(jnp.int32, (2 * tokens, 1), 0), tokens)
        ones[p] = one_zero(slot == over)
    row_i = lax.broadcasted_iota(jnp.int32, (tokens, 2 * tokens), 0)
    col_i = lax.broadcasted_iota(jnp.int32, (tokens, 2 * tokens), 1)
    same = lax.rem(row_i, places) == lax.rem(col_i, places)

    for c in range(CHUNKS):
        carry = None
        for g in range(groups):
            a, b = MID_CUTS[g], MID_CUTS[g + 1]
            if c == 0:
                for load in wq_loads[3 * g : 3 * g + 3]:
                    load.wait()
            if g == 0:
                all_copies(xs.at[c], xr.at[c], s1.at[c], r1.at[c], 0, model).wait_recv()
                part = xr[c].astype(F32).reshape(tokens, model).astype(BF16)
            weights = wq_parts[g]
            width = b - a
            for col in range(0, 3 * width, STEP):
                end = min(col + STEP, 3 * width)
                product = jnp.dot(part, weights[:, col:end], preferred_element_type=F32)
                for tile in range(col, end, LANES):
                    to = tile // width * model + a + tile % width
                    acc[:, to : to + LANES] = product[:, tile - col : tile - col + LANES]

            span = range(PAIR_CUTS[g], PAIR_CUTS[g + 1])
            k_sums, q_sums, scores, probs, tops, totals = {}, {}, {}, {}, {}, {}
            for p in span:
                lo, hi = p * LANES, p * LANES + WINDOW
                query = acc[:, lo:hi]
                keys = acc[:, model + lo : model + hi]
                sums = lax.dot_general(
                    key_rows[p],
                    (keys * keys).astype(BF16),
                    (((1,), (1,)), ((), ())),
                    preferred_element_type=F32,
                )
                k_sums[p] = jnp.concatenate([sums[0:1], sums[1:2]], axis=1)
                q_sums[p] = jnp.dot(
                    (query * query).astype(BF16), query_sum[p], preferred_element_type=F32
                )
            for p in span:
                lo, hi = p * LANES, p * LANES + WINDOW
                over = head_of((1, WINDOW), 1, p)
                keys = acc[:, model + lo : model + hi]
                keys = keys * gain[:, lo:hi]
                keys = jnp.concatenate(
                    [jnp.where(over == 0, keys, 0.0), jnp.where(over == 1, keys, 0.0)], axis=0
                ).astype(BF16)
                scores[p] = lax.dot_general(
                    acc[:, lo:hi].astype(BF16),
                    keys,
                    (((1,), (1,)), ((), ())),
                    preferred_element_type=F32,
                )
            for p in span:
                scaled = scores[p] * lax.rsqrt(q_sums[p] * (1.0 / HEAD_DIM) + 1e-06)
                scaled = scaled * lax.rsqrt(k_sums[p] * (1.0 / HEAD_DIM) + 1e-06)
                probs[p] = jnp.where(same, jnp.exp2(scaled), 0.0).astype(BF16)
            for p in span:
                lo, hi = p * LANES, p * LANES + WINDOW
                over = head_of((1, WINDOW), 1, p)
                vals = acc[:, 2 * model + lo : 2 * model + hi]
                vals = jnp.concatenate(
                    [jnp.where(over == 0, vals, 0.0), jnp.where(over == 1, vals, 0.0)], axis=0
                ).astype(BF16)
                tops[p] = jnp.dot(probs[p], vals, preferred_element_type=F32)
                totals[p] = jnp.dot(probs[p], ones[p], preferred_element_type=F32)
            for p in span:
                lo = p * LANES
                top, total = tops[p][:, :LANES], totals[p][:, :LANES]
                if carry is not None:
                    top, total = top + carry[0], total + carry[1]
                ys[c, :, :, lo : lo + LANES] = (top / total).reshape(n, places, LANES).astype(BF16)
                carry = (tops[p][:, LANES:], totals[p][:, LANES:])
            if g == groups - 1:
                done = carry[0] / carry[1]
                ys[c, :, :, model - LANES :] = done.reshape(n, places, LANES).astype(BF16)
            a, b = OUT_CUTS[g], OUT_CUTS[g + 1]
            send_all(ys.at[c], yr.at[c], s2.at[c, g], r2.at[c, g], a, b, ascending)
        yr[c, pl.ds(me, 1)] = ys[c, pl.ds(me, 1)]

    load_out.wait()
    for c in range(CHUNKS):
        all_copies(xs.at[c], xr.at[c], s1.at[c], r1.at[c], 0, model).wait_send()
    for c in range(CHUNKS):
        piece = pl.ds(c * half_rows, half_rows)
        branch = lat[c * half_rows : (c + 1) * half_rows].astype(F32).reshape(tokens, model)
        for g in range(groups):
            a, b = OUT_CUTS[g], OUT_CUTS[g + 1]
            all_copies(ys.at[c], yr.at[c], s2.at[c, g], r2.at[c, g], a, b).wait_recv()
            part = yr[c, :, :, a:b].astype(F32).reshape(tokens, b - a).astype(BF16)
            product = jnp.dot(part, wo[a:b, :], preferred_element_type=F32)
            out_ref[piece] = (branch + product).reshape(half_rows, columns, model).astype(BF16)
    for c in range(CHUNKS):
        for g in range(groups):
            a, b = OUT_CUTS[g], OUT_CUTS[g + 1]
            all_copies(ys.at[c], yr.at[c], s2.at[c, g], r2.at[c, g], a, b).wait_send()


def fused(n, latent, ln_gain, q_gain, k_gain, w_qkv, w_out):
    rows, columns, model = latent.shape
    places = rows * columns // (n * CHUNKS)
    tokens = n * places
    vmem = pl.BlockSpec(memory_space=pltpu.VMEM)
    hbm = pl.BlockSpec(memory_space=pltpu.HBM)
    block = pltpu.VMEM((CHUNKS, n, places, model), BF16)
    groups = len(MID_CUTS) - 1
    pairs = HEADS // 2
    dma = pltpu.SemaphoreType.DMA
    return pl.pallas_call(
        functools.partial(kernel, n),
        out_shape=jax.ShapeDtypeStruct(latent.shape, BF16),
        in_specs=[hbm] * 6,
        out_specs=vmem,
        scratch_shapes=[
            pltpu.VMEM(latent.shape, BF16),
            pltpu.VMEM(ln_gain.shape, F32),
            pltpu.VMEM(q_gain.shape, F32),
            pltpu.VMEM(k_gain.shape, F32),
            block,
            block,
            block,
            block,
            pltpu.VMEM((model, 3 * (MID_CUTS[1] - MID_CUTS[0])), BF16),
            pltpu.VMEM(w_out.shape, BF16),
            pltpu.VMEM((tokens, w_qkv.shape[1]), F32),
            pltpu.VMEM((pairs, KEY_ROWS, WINDOW), BF16),
            pltpu.VMEM((pairs, WINDOW, 2 * tokens), BF16),
            pltpu.VMEM((pairs, 2 * tokens, WINDOW), BF16),
            dma((CHUNKS,)),
            dma((3,)),
            dma((groups, 3)),
            dma,
            dma((CHUNKS,)),
            dma((CHUNKS,)),
            dma((CHUNKS, groups)),
            dma((CHUNKS, groups)),
            pltpu.SemaphoreType.REGULAR((n // PLANE,)),
        ],
        compiler_params=pltpu.CompilerParams(
            collective_id=0, has_side_effects=True, vmem_limit_bytes=VMEM_BYTES
        ),
    )(
        *(
            pltpu.with_memory_space_constraint(value, pltpu.HBM)
            for value in (latent, ln_gain, q_gain, k_gain, w_qkv, w_out)
        )
    )


def layer_norm(rows, ln_gain):
    values = rows.astype(jnp.float32)
    center = values - jnp.mean(values, axis=-1, keepdims=True)
    spread = jnp.mean(center * center, axis=-1, keepdims=True)
    return (center * lax.rsqrt(spread + 1e-06) * ln_gain).astype(jnp.bfloat16)


def head_norm(values, gain):
    shaped = values.reshape(values.shape[:-1] + (HEADS, HEAD_DIM))
    mean_sq = jnp.mean(shaped * shaped, axis=-1, keepdims=True)
    return (shaped * lax.rsqrt(mean_sq + 1e-06) * gain).astype(jnp.bfloat16).reshape(values.shape)


def project(normed, w_qkv, q_gain, k_gain):
    width = normed.shape[-1]
    mixed = jnp.dot(normed.reshape(-1, width), w_qkv, preferred_element_type=jnp.float32)
    mixed = mixed.reshape(normed.shape[:-1] + (3 * width,))
    query = head_norm(mixed[..., :width], q_gain)
    keys = head_norm(mixed[..., width : 2 * width], k_gain)
    values = mixed[..., 2 * width :].astype(jnp.bfloat16)
    return (query, keys, values)


def attend(query, keys, values):
    lead = query.shape[0]
    others = query.shape[1]
    q_four = query.reshape(lead, others, HEADS, HEAD_DIM)
    k_four = keys.reshape(lead, others, HEADS, HEAD_DIM)
    v_four = values.reshape(lead, others, HEADS, HEAD_DIM)
    scores = jnp.einsum(
        "tshe,ushe->shtu", q_four, k_four, preferred_element_type=jnp.float32
    ) * HEAD_DIM ** (-0.5)
    weights = jnp.exp(scores)
    weights = (weights / jnp.sum(weights, axis=-1, keepdims=True)).astype(jnp.bfloat16)
    mixed = jnp.einsum("shtu,ushe->tshe", weights, v_four, preferred_element_type=jnp.float32)
    return mixed.astype(jnp.bfloat16).reshape(query.shape)


def body(latent, ln_gain, q_gain, k_gain, w_qkv, w_out):
    device_count = lax.axis_size("frame")
    rows, columns, model = latent.shape
    positions = rows * columns
    per_peer = positions // device_count
    if per_peer % 8 == 0 and rows % CHUNKS == 0 and device_count % PLANE == 0:
        return fused(device_count, latent, ln_gain, q_gain, k_gain, w_qkv, w_out)
    flat = latent.reshape(positions, model)
    normed = layer_norm(flat, ln_gain)
    query, keys, values = project(
        lax.all_to_all(
            normed.reshape(device_count, per_peer, model),
            "frame",
            split_axis=0,
            concat_axis=0,
            tiled=True,
        ),
        w_qkv,
        q_gain,
        k_gain,
    )
    mixed = attend(query, keys, values)
    returned = lax.all_to_all(mixed, "frame", split_axis=0, concat_axis=0, tiled=True)
    attended = returned.reshape(positions, model)
    branch = jnp.dot(attended, w_out, preferred_element_type=jnp.float32)
    result = flat.astype(jnp.float32) + branch
    return result.astype(jnp.bfloat16).reshape(latent.shape)


def solution(mesh):
    placed = (P(("groups", "frame"), None, None), P(), P(), P(), P(), P())
    return jax.shard_map(
        body,
        mesh=mesh,
        in_specs=placed,
        out_specs=P(("groups", "frame"), None, None),
        check_vma=False,
    )
```

```python
import functools

import jax
import jax.numpy as jnp
from jax import lax
from jax.experimental import pallas as pl
from jax.experimental.pallas import tpu as pltpu
from jax.sharding import PartitionSpec as P

HEADS = 16
HEAD_DIM = 72
LANES = 128
WINDOW = 256
CHUNKS = 2
MID_CUTS = (0, 1152)
OUT_CUTS = (0, 1152)
PAIR_CUTS = (0, 8)
PLANE = 4
KEY_ROWS = 16
STEP = 256
VMEM_BYTES = 30000000
MESH = pl.DeviceIdType.MESH
F32 = jnp.float32
BF16 = jnp.bfloat16
LOG2_E = 1.4426950408889634


def kernel(
    n,
    lat_hbm,
    ln_hbm,
    qg_hbm,
    kg_hbm,
    wq_hbm,
    wo_hbm,
    out_ref,
    lat,
    ln_ref,
    qg_ref,
    kg_ref,
    xs,
    xr,
    ys,
    yr,
    wq0,
    wo,
    acc,
    key_rows,
    query_sum,
    ones,
    lat_sem,
    gain_sem,
    wq_sem,
    wo_sem,
    s1,
    r1,
    s2,
    r2,
    ready,
):
    rows, columns, model = lat_hbm.shape
    places = rows * columns // (n * CHUNKS)
    tokens = n * places
    half_rows = rows // CHUNKS
    groups = len(MID_CUTS) - 1
    pairs = HEADS // 2
    me = lax.axis_index("frame")
    planes = n // PLANE
    depth = lax.div(me, PLANE)
    spot = lax.rem(me, PLANE)
    turn = [lax.rem(spot + k, PLANE) for k in range(PLANE)]
    ascending = [k + (me <= k).astype(jnp.int32) for k in range(n - 1)]
    half = n // 2
    beyond = [half + lax.rem(to + PLANE, half) for to in ascending]
    farthest = [
        jnp.where(jnp.logical_and(me < half, to >= half), other, to)
        for to, other in zip(ascending, beyond)
    ]

    def tell(semaphore, to):
        pl.semaphore_signal(semaphore, inc=1, device_id={"frame": to}, device_id_type=MESH)

    lat_loads = []
    for c in range(CHUNKS):
        part = pl.ds(c * half_rows, half_rows)
        lat_loads.append(pltpu.make_async_copy(lat_hbm.at[part], lat.at[part], lat_sem.at[c]))
    gains = [
        pltpu.make_async_copy(src, dst, gain_sem.at[i])
        for i, (src, dst) in enumerate(((ln_hbm, ln_ref), (qg_hbm, qg_ref), (kg_hbm, kg_ref)))
    ]
    for load in (lat_loads[0], gains[0], lat_loads[1], gains[1], gains[2]):
        load.start()

    for plane in range(planes - 1, 0, -1):

        @pl.when(depth < plane)
        def _():
            for t in turn:
                tell(pltpu.get_barrier_semaphore(), plane * PLANE + t)

    for k in range(1, PLANE):

        @pl.when(spot + k < PLANE)
        def _():
            tell(pltpu.get_barrier_semaphore(), me + k)

    wq_parts = (wq0,)
    wq_loads = []
    for g in range(groups):
        a, b = MID_CUTS[g], MID_CUTS[g + 1]
        for third in range(3):
            load = pltpu.make_async_copy(
                wq_hbm.at[:, pl.ds(third * model + a, b - a)],
                wq_parts[g].at[:, pl.ds(third * (b - a), b - a)],
                wq_sem.at[g, third],
            )
            wq_loads.append(load)
    load_out = pltpu.make_async_copy(wo_hbm, wo, wo_sem)

    def send_all(src, dst, send, recv, a, b, order):
        for to in order:
            pltpu.make_async_remote_copy(
                src_ref=src.at[to, :, pl.ds(a, b - a)],
                dst_ref=dst.at[me, :, pl.ds(a, b - a)],
                send_sem=send,
                recv_sem=recv,
                device_id={"frame": to},
                device_id_type=MESH,
            ).start()

    def all_copies(src, dst, send, recv, a, b):
        return pltpu.make_async_remote_copy(
            src_ref=src.at[pl.ds(0, n - 1), :, pl.ds(a, b - a)],
            dst_ref=dst.at[pl.ds(0, n - 1), :, pl.ds(a, b - a)],
            send_sem=send,
            recv_sem=recv,
            device_id={"frame": ascending[0]},
            device_id_type=MESH,
        )

    def normalize(c):
        lat_loads[c].wait()
        block = lat[c * half_rows : (c + 1) * half_rows]
        values = block.astype(F32).reshape(tokens, model)
        center = values - jnp.mean(values, axis=-1, keepdims=True)
        spread = jnp.mean(center * center, axis=-1, keepdims=True)
        normed = center * lax.rsqrt(spread + 1e-06) * ln_ref[...].reshape(1, model)
        xs[c] = normed.reshape(n, places, model).astype(BF16)

    def send_normed(c, order):
        send_all(xs.at[c], xr.at[c], s1.at[c], r1.at[c], 0, model, order)

    @pl.when(me > 0)
    def _():
        pl.semaphore_wait(pltpu.get_barrier_semaphore(), me)

    for plane in range(planes - 1):

        @pl.when(plane < depth)
        def _():
            for t in turn:
                tell(ready.at[depth], plane * PLANE + t)

    for k in range(1, PLANE):

        @pl.when(spot >= k)
        def _():
            tell(ready.at[depth], me - k)

    gains[0].wait()
    normalize(0)
    for plane in range(planes):
        if plane == planes - 1:
            normalize(1)
        missing = jnp.where(plane > depth, PLANE, jnp.where(plane == depth, PLANE - 1 - spot, 0))

        @pl.when(missing > 0)
        def _():
            pl.semaphore_wait(ready.at[plane], missing)

        @pl.when(plane != depth)
        def _():
            send_normed(0, [plane * PLANE + turn[0]])

        send_normed(0, [plane * PLANE + t for t in turn[1:]])
    send_normed(1, farthest)
    for load in wq_loads:
        load.start()
    load_out.start()
    for c in range(CHUNKS):
        xr[c, pl.ds(me, 1)] = xs[c, pl.ds(me, 1)]

    gains[1].wait()
    gains[2].wait()
    entry = lax.broadcasted_iota(jnp.int32, (HEAD_DIM, model), 0)
    place = lax.broadcasted_iota(jnp.int32, (HEAD_DIM, model), 1)
    repeat = (lax.rem(place, HEAD_DIM) == entry).astype(F32)
    both = qg_ref[...] * kg_ref[...] * (HEAD_DIM**-0.5 * LOG2_E)
    gain = jnp.dot(
        jnp.broadcast_to(both.reshape(1, HEAD_DIM), (8, HEAD_DIM)),
        repeat,
        preferred_element_type=F32,
        precision=lax.Precision.HIGHEST,
    )[0:1]

    def head_of(shape, axis, p):
        lane = lax.broadcasted_iota(jnp.int32, shape, axis) + (p * LANES - 2 * p * HEAD_DIM)
        return jnp.where(lane < 0, -1, jnp.where(lane < HEAD_DIM, 0, jnp.where(lane < 2 * HEAD_DIM, 1, 2)))

    def one_zero(mask):
        return jnp.where(mask, 1.0, 0.0).astype(BF16)

    for p in range(pairs):
        down = head_of((WINDOW, 1), 0, p)
        over = head_of((1, WINDOW), 1, p)
        key_rows[p] = one_zero(lax.broadcasted_iota(jnp.int32, (KEY_ROWS, 1), 0) == over)
        slot = lax.div(lax.broadcasted_iota(jnp.int32, (1, 2 * tokens), 1), tokens)
        query_sum[p] = one_zero(down == slot)
        slot = lax.div(lax.broadcasted_iota(jnp.int32, (2 * tokens, 1), 0), tokens)
        ones[p] = one_zero(slot == over)
    row_i = lax.broadcasted_iota(jnp.int32, (tokens, 2 * tokens), 0)
    col_i = lax.broadcasted_iota(jnp.int32, (tokens, 2 * tokens), 1)
    same = lax.rem(row_i, places) == lax.rem(col_i, places)

    for c in range(CHUNKS):
        carry = None
        for g in range(groups):
            a, b = MID_CUTS[g], MID_CUTS[g + 1]
            if c == 0:
                for load in wq_loads[3 * g : 3 * g + 3]:
                    load.wait()
            if g == 0:
                all_copies(xs.at[c], xr.at[c], s1.at[c], r1.at[c], 0, model).wait_recv()
                part = xr[c].astype(F32).reshape(tokens, model).astype(BF16)
            weights = wq_parts[g]
            width = b - a
            for col in range(0, 3 * width, STEP):
                end = min(col + STEP, 3 * width)
                product = jnp.dot(part, weights[:, col:end], preferred_element_type=F32)
                for tile in range(col, end, LANES):
                    to = tile // width * model + a + tile % width
                    acc[:, to : to + LANES] = product[:, tile - col : tile - col + LANES]

            span = range(PAIR_CUTS[g], PAIR_CUTS[g + 1])
            k_sums, q_sums, scores, probs, tops, totals = {}, {}, {}, {}, {}, {}
            for p in span:
                lo, hi = p * LANES, p * LANES + WINDOW
                query = acc[:, lo:hi]
                keys = acc[:, model + lo : model + hi]
                sums = lax.dot_general(
                    key_rows[p],
                    (keys * keys).astype(BF16),
                    (((1,), (1,)), ((), ())),
                    preferred_element_type=F32,
                )
                k_sums[p] = jnp.concatenate([sums[0:1], sums[1:2]], axis=1)
                q_sums[p] = jnp.dot(
                    (query * query).astype(BF16), query_sum[p], preferred_element_type=F32
                )
            for p in span:
                lo, hi = p * LANES, p * LANES + WINDOW
                over = head_of((1, WINDOW), 1, p)
                keys = acc[:, model + lo : model + hi]
                keys = keys * gain[:, lo:hi]
                keys = jnp.concatenate(
                    [jnp.where(over == 0, keys, 0.0), jnp.where(over == 1, keys, 0.0)], axis=0
                ).astype(BF16)
                scores[p] = lax.dot_general(
                    acc[:, lo:hi].astype(BF16),
                    keys,
                    (((1,), (1,)), ((), ())),
                    preferred_element_type=F32,
                )
            for p in span:
                scaled = scores[p] * lax.rsqrt(q_sums[p] * (1.0 / HEAD_DIM) + 1e-06)
                scaled = scaled * lax.rsqrt(k_sums[p] * (1.0 / HEAD_DIM) + 1e-06)
                probs[p] = jnp.where(same, jnp.exp2(scaled), 0.0).astype(BF16)
            for p in span:
                lo, hi = p * LANES, p * LANES + WINDOW
                over = head_of((1, WINDOW), 1, p)
                vals = acc[:, 2 * model + lo : 2 * model + hi]
                vals = jnp.concatenate(
                    [jnp.where(over == 0, vals, 0.0), jnp.where(over == 1, vals, 0.0)], axis=0
                ).astype(BF16)
                tops[p] = jnp.dot(probs[p], vals, preferred_element_type=F32)
                totals[p] = jnp.dot(probs[p], ones[p], preferred_element_type=F32)
            for p in span:
                lo = p * LANES
                top, total = tops[p][:, :LANES], totals[p][:, :LANES]
                if carry is not None:
                    top, total = top + carry[0], total + carry[1]
                ys[c, :, :, lo : lo + LANES] = (top / total).reshape(n, places, LANES).astype(BF16)
                carry = (tops[p][:, LANES:], totals[p][:, LANES:])
            if g == groups - 1:
                done = carry[0] / carry[1]
                ys[c, :, :, model - LANES :] = done.reshape(n, places, LANES).astype(BF16)
            a, b = OUT_CUTS[g], OUT_CUTS[g + 1]
            send_all(ys.at[c], yr.at[c], s2.at[c, g], r2.at[c, g], a, b, ascending)
        yr[c, pl.ds(me, 1)] = ys[c, pl.ds(me, 1)]

    load_out.wait()
    for c in range(CHUNKS):
        all_copies(xs.at[c], xr.at[c], s1.at[c], r1.at[c], 0, model).wait_send()
    for c in range(CHUNKS):
        piece = pl.ds(c * half_rows, half_rows)
        branch = lat[c * half_rows : (c + 1) * half_rows].astype(F32).reshape(tokens, model)
        for g in range(groups):
            a, b = OUT_CUTS[g], OUT_CUTS[g + 1]
            all_copies(ys.at[c], yr.at[c], s2.at[c, g], r2.at[c, g], a, b).wait_recv()
            part = yr[c, :, :, a:b].astype(F32).reshape(tokens, b - a).astype(BF16)
            product = jnp.dot(part, wo[a:b, :], preferred_element_type=F32)
            out_ref[piece] = (branch + product).reshape(half_rows, columns, model).astype(BF16)
    for c in range(CHUNKS):
        for g in range(groups):
            a, b = OUT_CUTS[g], OUT_CUTS[g + 1]
            all_copies(ys.at[c], yr.at[c], s2.at[c, g], r2.at[c, g], a, b).wait_send()


def fused(n, latent, ln_gain, q_gain, k_gain, w_qkv, w_out):
    rows, columns, model = latent.shape
    places = rows * columns // (n * CHUNKS)
    tokens = n * places
    vmem = pl.BlockSpec(memory_space=pltpu.VMEM)
    hbm = pl.BlockSpec(memory_space=pltpu.HBM)
    block = pltpu.VMEM((CHUNKS, n, places, model), BF16)
    groups = len(MID_CUTS) - 1
    pairs = HEADS // 2
    dma = pltpu.SemaphoreType.DMA
    return pl.pallas_call(
        functools.partial(kernel, n),
        out_shape=jax.ShapeDtypeStruct(latent.shape, BF16),
        in_specs=[hbm] * 6,
        out_specs=vmem,
        scratch_shapes=[
            pltpu.VMEM(latent.shape, BF16),
            pltpu.VMEM(ln_gain.shape, F32),
            pltpu.VMEM(q_gain.shape, F32),
            pltpu.VMEM(k_gain.shape, F32),
            block,
            block,
            block,
            block,
            pltpu.VMEM((model, 3 * (MID_CUTS[1] - MID_CUTS[0])), BF16),
            pltpu.VMEM(w_out.shape, BF16),
            pltpu.VMEM((tokens, w_qkv.shape[1]), F32),
            pltpu.VMEM((pairs, KEY_ROWS, WINDOW), BF16),
            pltpu.VMEM((pairs, WINDOW, 2 * tokens), BF16),
            pltpu.VMEM((pairs, 2 * tokens, WINDOW), BF16),
            dma((CHUNKS,)),
            dma((3,)),
            dma((groups, 3)),
            dma,
            dma((CHUNKS,)),
            dma((CHUNKS,)),
            dma((CHUNKS, groups)),
            dma((CHUNKS, groups)),
            pltpu.SemaphoreType.REGULAR((n // PLANE,)),
        ],
        compiler_params=pltpu.CompilerParams(
            collective_id=0, has_side_effects=True, vmem_limit_bytes=VMEM_BYTES
        ),
    )(
        *(
            pltpu.with_memory_space_constraint(value, pltpu.HBM)
            for value in (latent, ln_gain, q_gain, k_gain, w_qkv, w_out)
        )
    )


def layer_norm(rows, ln_gain):
    values = rows.astype(jnp.float32)
    center = values - jnp.mean(values, axis=-1, keepdims=True)
    spread = jnp.mean(center * center, axis=-1, keepdims=True)
    return (center * lax.rsqrt(spread + 1e-06) * ln_gain).astype(jnp.bfloat16)


def head_norm(values, gain):
    shaped = values.reshape(values.shape[:-1] + (HEADS, HEAD_DIM))
    mean_sq = jnp.mean(shaped * shaped, axis=-1, keepdims=True)
    return (shaped * lax.rsqrt(mean_sq + 1e-06) * gain).astype(jnp.bfloat16).reshape(values.shape)


def project(normed, w_qkv, q_gain, k_gain):
    width = normed.shape[-1]
    mixed = jnp.dot(normed.reshape(-1, width), w_qkv, preferred_element_type=jnp.float32)
    mixed = mixed.reshape(normed.shape[:-1] + (3 * width,))
    query = head_norm(mixed[..., :width], q_gain)
    keys = head_norm(mixed[..., width : 2 * width], k_gain)
    values = mixed[..., 2 * width :].astype(jnp.bfloat16)
    return (query, keys, values)


def attend(query, keys, values):
    lead = query.shape[0]
    others = query.shape[1]
    q_four = query.reshape(lead, others, HEADS, HEAD_DIM)
    k_four = keys.reshape(lead, others, HEADS, HEAD_DIM)
    v_four = values.reshape(lead, others, HEADS, HEAD_DIM)
    scores = jnp.einsum(
        "tshe,ushe->shtu", q_four, k_four, preferred_element_type=jnp.float32
    ) * HEAD_DIM ** (-0.5)
    weights = jnp.exp(scores)
    weights = (weights / jnp.sum(weights, axis=-1, keepdims=True)).astype(jnp.bfloat16)
    mixed = jnp.einsum("shtu,ushe->tshe", weights, v_four, preferred_element_type=jnp.float32)
    return mixed.astype(jnp.bfloat16).reshape(query.shape)


def body(latent, ln_gain, q_gain, k_gain, w_qkv, w_out):
    device_count = lax.axis_size("frame")
    rows, columns, model = latent.shape
    positions = rows * columns
    per_peer = positions // device_count
    if per_peer % 8 == 0 and rows % CHUNKS == 0 and device_count % PLANE == 0:
        return fused(device_count, latent, ln_gain, q_gain, k_gain, w_qkv, w_out)
    flat = latent.reshape(positions, model)
    normed = layer_norm(flat, ln_gain)
    query, keys, values = project(
        lax.all_to_all(
            normed.reshape(device_count, per_peer, model),
            "frame",
            split_axis=0,
            concat_axis=0,
            tiled=True,
        ),
        w_qkv,
        q_gain,
        k_gain,
    )
    mixed = attend(query, keys, values)
    returned = lax.all_to_all(mixed, "frame", split_axis=0, concat_axis=0, tiled=True)
    attended = returned.reshape(positions, model)
    branch = jnp.dot(attended, w_out, preferred_element_type=jnp.float32)
    result = flat.astype(jnp.float32) + branch
    return result.astype(jnp.bfloat16).reshape(latent.shape)


def solution(mesh):
    placed = (P(("groups", "frame"), None, None), P(), P(), P(), P(), P())
    return jax.shard_map(
        body,
        mesh=mesh,
        in_specs=placed,
        out_specs=P(("groups", "frame"), None, None),
        check_vma=False,
    )
```

```python
import functools

import jax
import jax.numpy as jnp
from jax import lax
from jax.experimental import pallas as pl
from jax.experimental.pallas import tpu as pltpu
from jax.sharding import PartitionSpec as P

HEADS = 16
HEAD_DIM = 72
LANES = 128
WINDOW = 256
CHUNKS = 2
MID_CUTS = (0, 1152)
OUT_CUTS = (0, 1152)
PAIR_CUTS = (0, 8)
PLANE = 4
KEY_ROWS = 16
STEP = 256
VMEM_BYTES = 30000000
MESH = pl.DeviceIdType.MESH
F32 = jnp.float32
BF16 = jnp.bfloat16
LOG2_E = 1.4426950408889634


def kernel(
    n,
    lat_hbm,
    ln_hbm,
    qg_hbm,
    kg_hbm,
    wq_hbm,
    wo_hbm,
    out_ref,
    lat,
    ln_ref,
    qg_ref,
    kg_ref,
    xs,
    xr,
    ys,
    yr,
    wq0,
    wo,
    acc,
    key_rows,
    query_sum,
    ones,
    lat_sem,
    gain_sem,
    wq_sem,
    wo_sem,
    s1,
    r1,
    s2,
    r2,
    ready,
):
    rows, columns, model = lat_hbm.shape
    places = rows * columns // (n * CHUNKS)
    tokens = n * places
    half_rows = rows // CHUNKS
    groups = len(MID_CUTS) - 1
    pairs = HEADS // 2
    me = lax.axis_index("frame")
    planes = n // PLANE
    depth = lax.div(me, PLANE)
    spot = lax.rem(me, PLANE)
    turn = [lax.rem(spot + k, PLANE) for k in range(PLANE)]
    ascending = [k + (me <= k).astype(jnp.int32) for k in range(n - 1)]

    def tell(semaphore, to):
        pl.semaphore_signal(semaphore, inc=1, device_id={"frame": to}, device_id_type=MESH)

    lat_loads = []
    for c in range(CHUNKS):
        part = pl.ds(c * half_rows, half_rows)
        lat_loads.append(pltpu.make_async_copy(lat_hbm.at[part], lat.at[part], lat_sem.at[c]))
    gains = [
        pltpu.make_async_copy(src, dst, gain_sem.at[i])
        for i, (src, dst) in enumerate(((ln_hbm, ln_ref), (qg_hbm, qg_ref), (kg_hbm, kg_ref)))
    ]
    for load in (lat_loads[0], gains[0], lat_loads[1], gains[1], gains[2]):
        load.start()

    for plane in range(planes - 1, 0, -1):

        @pl.when(depth < plane)
        def _():
            for t in turn:
                tell(pltpu.get_barrier_semaphore(), plane * PLANE + t)

    for k in range(1, PLANE):

        @pl.when(spot + k < PLANE)
        def _():
            tell(pltpu.get_barrier_semaphore(), me + k)

    wq_parts = (wq0,)
    wq_loads = []
    for g in range(groups):
        a, b = MID_CUTS[g], MID_CUTS[g + 1]
        for third in range(3):
            load = pltpu.make_async_copy(
                wq_hbm.at[:, pl.ds(third * model + a, b - a)],
                wq_parts[g].at[:, pl.ds(third * (b - a), b - a)],
                wq_sem.at[g, third],
            )
            wq_loads.append(load)
    load_out = pltpu.make_async_copy(wo_hbm, wo, wo_sem)

    def send_all(src, dst, send, recv, a, b, order):
        for to in order:
            pltpu.make_async_remote_copy(
                src_ref=src.at[to, :, pl.ds(a, b - a)],
                dst_ref=dst.at[me, :, pl.ds(a, b - a)],
                send_sem=send,
                recv_sem=recv,
                device_id={"frame": to},
                device_id_type=MESH,
            ).start()

    def all_copies(src, dst, send, recv, a, b):
        return pltpu.make_async_remote_copy(
            src_ref=src.at[pl.ds(0, n - 1), :, pl.ds(a, b - a)],
            dst_ref=dst.at[pl.ds(0, n - 1), :, pl.ds(a, b - a)],
            send_sem=send,
            recv_sem=recv,
            device_id={"frame": ascending[0]},
            device_id_type=MESH,
        )

    def normalize(c):
        lat_loads[c].wait()
        block = lat[c * half_rows : (c + 1) * half_rows]
        values = block.astype(F32).reshape(tokens, model)
        center = values - jnp.mean(values, axis=-1, keepdims=True)
        spread = jnp.mean(center * center, axis=-1, keepdims=True)
        normed = center * lax.rsqrt(spread + 1e-06) * ln_ref[...].reshape(1, model)
        xs[c] = normed.reshape(n, places, model).astype(BF16)

    def send_normed(c, order):
        send_all(xs.at[c], xr.at[c], s1.at[c], r1.at[c], 0, model, order)

    @pl.when(me > 0)
    def _():
        pl.semaphore_wait(pltpu.get_barrier_semaphore(), me)

    for plane in range(planes - 1):

        @pl.when(plane < depth)
        def _():
            for t in turn:
                tell(ready.at[depth], plane * PLANE + t)

    for k in range(1, PLANE):

        @pl.when(spot >= k)
        def _():
            tell(ready.at[depth], me - k)

    def load_weights():
        for load in wq_loads:
            load.start()
        load_out.start()

    @pl.when(depth < planes // 2)
    def _():
        load_weights()

    gains[0].wait()
    normalize(0)
    for plane in range(planes):
        if plane == planes - 1:
            normalize(1)
        missing = jnp.where(plane > depth, PLANE, jnp.where(plane == depth, PLANE - 1 - spot, 0))

        @pl.when(missing > 0)
        def _():
            pl.semaphore_wait(ready.at[plane], missing)

        @pl.when(plane != depth)
        def _():
            send_normed(0, [plane * PLANE + turn[0]])

        send_normed(0, [plane * PLANE + t for t in turn[1:]])
    send_normed(1, ascending)
    @pl.when(depth >= planes // 2)
    def _():
        load_weights()

    for c in range(CHUNKS):
        xr[c, pl.ds(me, 1)] = xs[c, pl.ds(me, 1)]

    gains[1].wait()
    gains[2].wait()
    entry = lax.broadcasted_iota(jnp.int32, (HEAD_DIM, model), 0)
    place = lax.broadcasted_iota(jnp.int32, (HEAD_DIM, model), 1)
    repeat = (lax.rem(place, HEAD_DIM) == entry).astype(F32)
    both = qg_ref[...] * kg_ref[...] * (HEAD_DIM**-0.5 * LOG2_E)
    gain = jnp.dot(
        jnp.broadcast_to(both.reshape(1, HEAD_DIM), (8, HEAD_DIM)),
        repeat,
        preferred_element_type=F32,
        precision=lax.Precision.HIGHEST,
    )[0:1]

    def head_of(shape, axis, p):
        lane = lax.broadcasted_iota(jnp.int32, shape, axis) + (p * LANES - 2 * p * HEAD_DIM)
        return jnp.where(lane < 0, -1, jnp.where(lane < HEAD_DIM, 0, jnp.where(lane < 2 * HEAD_DIM, 1, 2)))

    def one_zero(mask):
        return jnp.where(mask, 1.0, 0.0).astype(BF16)

    for p in range(pairs):
        down = head_of((WINDOW, 1), 0, p)
        over = head_of((1, WINDOW), 1, p)
        key_rows[p] = one_zero(lax.broadcasted_iota(jnp.int32, (KEY_ROWS, 1), 0) == over)
        slot = lax.div(lax.broadcasted_iota(jnp.int32, (1, 2 * tokens), 1), tokens)
        query_sum[p] = one_zero(down == slot)
        slot = lax.div(lax.broadcasted_iota(jnp.int32, (2 * tokens, 1), 0), tokens)
        ones[p] = one_zero(slot == over)
    row_i = lax.broadcasted_iota(jnp.int32, (tokens, 2 * tokens), 0)
    col_i = lax.broadcasted_iota(jnp.int32, (tokens, 2 * tokens), 1)
    same = lax.rem(row_i, places) == lax.rem(col_i, places)

    for c in range(CHUNKS):
        carry = None
        for g in range(groups):
            a, b = MID_CUTS[g], MID_CUTS[g + 1]
            if c == 0:
                for load in wq_loads[3 * g : 3 * g + 3]:
                    load.wait()
            if g == 0:
                all_copies(xs.at[c], xr.at[c], s1.at[c], r1.at[c], 0, model).wait_recv()
                part = xr[c].astype(F32).reshape(tokens, model).astype(BF16)
            weights = wq_parts[g]
            width = b - a
            for col in range(0, 3 * width, STEP):
                end = min(col + STEP, 3 * width)
                product = jnp.dot(part, weights[:, col:end], preferred_element_type=F32)
                for tile in range(col, end, LANES):
                    to = tile // width * model + a + tile % width
                    acc[:, to : to + LANES] = product[:, tile - col : tile - col + LANES]

            span = range(PAIR_CUTS[g], PAIR_CUTS[g + 1])
            k_sums, q_sums, scores, probs, tops, totals = {}, {}, {}, {}, {}, {}
            for p in span:
                lo, hi = p * LANES, p * LANES + WINDOW
                query = acc[:, lo:hi]
                keys = acc[:, model + lo : model + hi]
                sums = lax.dot_general(
                    key_rows[p],
                    (keys * keys).astype(BF16),
                    (((1,), (1,)), ((), ())),
                    preferred_element_type=F32,
                )
                k_sums[p] = jnp.concatenate([sums[0:1], sums[1:2]], axis=1)
                q_sums[p] = jnp.dot(
                    (query * query).astype(BF16), query_sum[p], preferred_element_type=F32
                )
            for p in span:
                lo, hi = p * LANES, p * LANES + WINDOW
                over = head_of((1, WINDOW), 1, p)
                keys = acc[:, model + lo : model + hi]
                keys = keys * gain[:, lo:hi]
                keys = jnp.concatenate(
                    [jnp.where(over == 0, keys, 0.0), jnp.where(over == 1, keys, 0.0)], axis=0
                ).astype(BF16)
                scores[p] = lax.dot_general(
                    acc[:, lo:hi].astype(BF16),
                    keys,
                    (((1,), (1,)), ((), ())),
                    preferred_element_type=F32,
                )
            for p in span:
                scaled = scores[p] * lax.rsqrt(q_sums[p] * (1.0 / HEAD_DIM) + 1e-06)
                scaled = scaled * lax.rsqrt(k_sums[p] * (1.0 / HEAD_DIM) + 1e-06)
                probs[p] = jnp.where(same, jnp.exp2(scaled), 0.0).astype(BF16)
            for p in span:
                lo, hi = p * LANES, p * LANES + WINDOW
                over = head_of((1, WINDOW), 1, p)
                vals = acc[:, 2 * model + lo : 2 * model + hi]
                vals = jnp.concatenate(
                    [jnp.where(over == 0, vals, 0.0), jnp.where(over == 1, vals, 0.0)], axis=0
                ).astype(BF16)
                tops[p] = jnp.dot(probs[p], vals, preferred_element_type=F32)
                totals[p] = jnp.dot(probs[p], ones[p], preferred_element_type=F32)
            for p in span:
                lo = p * LANES
                top, total = tops[p][:, :LANES], totals[p][:, :LANES]
                if carry is not None:
                    top, total = top + carry[0], total + carry[1]
                ys[c, :, :, lo : lo + LANES] = (top / total).reshape(n, places, LANES).astype(BF16)
                carry = (tops[p][:, LANES:], totals[p][:, LANES:])
            if g == groups - 1:
                done = carry[0] / carry[1]
                ys[c, :, :, model - LANES :] = done.reshape(n, places, LANES).astype(BF16)
            a, b = OUT_CUTS[g], OUT_CUTS[g + 1]
            send_all(ys.at[c], yr.at[c], s2.at[c, g], r2.at[c, g], a, b, ascending)
        yr[c, pl.ds(me, 1)] = ys[c, pl.ds(me, 1)]

    load_out.wait()
    for c in range(CHUNKS):
        all_copies(xs.at[c], xr.at[c], s1.at[c], r1.at[c], 0, model).wait_send()
    for c in range(CHUNKS):
        piece = pl.ds(c * half_rows, half_rows)
        branch = lat[c * half_rows : (c + 1) * half_rows].astype(F32).reshape(tokens, model)
        for g in range(groups):
            a, b = OUT_CUTS[g], OUT_CUTS[g + 1]
            all_copies(ys.at[c], yr.at[c], s2.at[c, g], r2.at[c, g], a, b).wait_recv()
            part = yr[c, :, :, a:b].astype(F32).reshape(tokens, b - a).astype(BF16)
            product = jnp.dot(part, wo[a:b, :], preferred_element_type=F32)
            out_ref[piece] = (branch + product).reshape(half_rows, columns, model).astype(BF16)
    for c in range(CHUNKS):
        for g in range(groups):
            a, b = OUT_CUTS[g], OUT_CUTS[g + 1]
            all_copies(ys.at[c], yr.at[c], s2.at[c, g], r2.at[c, g], a, b).wait_send()


def fused(n, latent, ln_gain, q_gain, k_gain, w_qkv, w_out):
    rows, columns, model = latent.shape
    places = rows * columns // (n * CHUNKS)
    tokens = n * places
    vmem = pl.BlockSpec(memory_space=pltpu.VMEM)
    hbm = pl.BlockSpec(memory_space=pltpu.HBM)
    block = pltpu.VMEM((CHUNKS, n, places, model), BF16)
    groups = len(MID_CUTS) - 1
    pairs = HEADS // 2
    dma = pltpu.SemaphoreType.DMA
    return pl.pallas_call(
        functools.partial(kernel, n),
        out_shape=jax.ShapeDtypeStruct(latent.shape, BF16),
        in_specs=[hbm] * 6,
        out_specs=vmem,
        scratch_shapes=[
            pltpu.VMEM(latent.shape, BF16),
            pltpu.VMEM(ln_gain.shape, F32),
            pltpu.VMEM(q_gain.shape, F32),
            pltpu.VMEM(k_gain.shape, F32),
            block,
            block,
            block,
            block,
            pltpu.VMEM((model, 3 * (MID_CUTS[1] - MID_CUTS[0])), BF16),
            pltpu.VMEM(w_out.shape, BF16),
            pltpu.VMEM((tokens, w_qkv.shape[1]), F32),
            pltpu.VMEM((pairs, KEY_ROWS, WINDOW), BF16),
            pltpu.VMEM((pairs, WINDOW, 2 * tokens), BF16),
            pltpu.VMEM((pairs, 2 * tokens, WINDOW), BF16),
            dma((CHUNKS,)),
            dma((3,)),
            dma((groups, 3)),
            dma,
            dma((CHUNKS,)),
            dma((CHUNKS,)),
            dma((CHUNKS, groups)),
            dma((CHUNKS, groups)),
            pltpu.SemaphoreType.REGULAR((n // PLANE,)),
        ],
        compiler_params=pltpu.CompilerParams(
            collective_id=0, has_side_effects=True, vmem_limit_bytes=VMEM_BYTES
        ),
    )(
        *(
            pltpu.with_memory_space_constraint(value, pltpu.HBM)
            for value in (latent, ln_gain, q_gain, k_gain, w_qkv, w_out)
        )
    )


def layer_norm(rows, ln_gain):
    values = rows.astype(jnp.float32)
    center = values - jnp.mean(values, axis=-1, keepdims=True)
    spread = jnp.mean(center * center, axis=-1, keepdims=True)
    return (center * lax.rsqrt(spread + 1e-06) * ln_gain).astype(jnp.bfloat16)


def head_norm(values, gain):
    shaped = values.reshape(values.shape[:-1] + (HEADS, HEAD_DIM))
    mean_sq = jnp.mean(shaped * shaped, axis=-1, keepdims=True)
    return (shaped * lax.rsqrt(mean_sq + 1e-06) * gain).astype(jnp.bfloat16).reshape(values.shape)


def project(normed, w_qkv, q_gain, k_gain):
    width = normed.shape[-1]
    mixed = jnp.dot(normed.reshape(-1, width), w_qkv, preferred_element_type=jnp.float32)
    mixed = mixed.reshape(normed.shape[:-1] + (3 * width,))
    query = head_norm(mixed[..., :width], q_gain)
    keys = head_norm(mixed[..., width : 2 * width], k_gain)
    values = mixed[..., 2 * width :].astype(jnp.bfloat16)
    return (query, keys, values)


def attend(query, keys, values):
    lead = query.shape[0]
    others = query.shape[1]
    q_four = query.reshape(lead, others, HEADS, HEAD_DIM)
    k_four = keys.reshape(lead, others, HEADS, HEAD_DIM)
    v_four = values.reshape(lead, others, HEADS, HEAD_DIM)
    scores = jnp.einsum(
        "tshe,ushe->shtu", q_four, k_four, preferred_element_type=jnp.float32
    ) * HEAD_DIM ** (-0.5)
    weights = jnp.exp(scores)
    weights = (weights / jnp.sum(weights, axis=-1, keepdims=True)).astype(jnp.bfloat16)
    mixed = jnp.einsum("shtu,ushe->tshe", weights, v_four, preferred_element_type=jnp.float32)
    return mixed.astype(jnp.bfloat16).reshape(query.shape)


def body(latent, ln_gain, q_gain, k_gain, w_qkv, w_out):
    device_count = lax.axis_size("frame")
    rows, columns, model = latent.shape
    positions = rows * columns
    per_peer = positions // device_count
    if per_peer % 8 == 0 and rows % CHUNKS == 0 and device_count % PLANE == 0:
        return fused(device_count, latent, ln_gain, q_gain, k_gain, w_qkv, w_out)
    flat = latent.reshape(positions, model)
    normed = layer_norm(flat, ln_gain)
    query, keys, values = project(
        lax.all_to_all(
            normed.reshape(device_count, per_peer, model),
            "frame",
            split_axis=0,
            concat_axis=0,
            tiled=True,
        ),
        w_qkv,
        q_gain,
        k_gain,
    )
    mixed = attend(query, keys, values)
    returned = lax.all_to_all(mixed, "frame", split_axis=0, concat_axis=0, tiled=True)
    attended = returned.reshape(positions, model)
    branch = jnp.dot(attended, w_out, preferred_element_type=jnp.float32)
    result = flat.astype(jnp.float32) + branch
    return result.astype(jnp.bfloat16).reshape(latent.shape)


def solution(mesh):
    placed = (P(("groups", "frame"), None, None), P(), P(), P(), P(), P())
    return jax.shard_map(
        body,
        mesh=mesh,
        in_specs=placed,
        out_specs=P(("groups", "frame"), None, None),
        check_vma=False,
    )
```

```python
import functools

import jax
import jax.numpy as jnp
from jax import lax
from jax.experimental import pallas as pl
from jax.experimental.pallas import tpu as pltpu
from jax.sharding import PartitionSpec as P

HEADS = 16
HEAD_DIM = 72
LANES = 128
WINDOW = 256
CHUNKS = 2
MID_CUTS = (0, 1152)
OUT_CUTS = (0, 1152)
PAIR_CUTS = (0, 8)
PLANE = 4
KEY_ROWS = 16
STEP = 256
VMEM_BYTES = 30000000
MESH = pl.DeviceIdType.MESH
F32 = jnp.float32
BF16 = jnp.bfloat16
LOG2_E = 1.4426950408889634


def kernel(
    n,
    lat_hbm,
    ln_hbm,
    qg_hbm,
    kg_hbm,
    wq_hbm,
    wo_hbm,
    out_ref,
    lat,
    ln_ref,
    qg_ref,
    kg_ref,
    xs,
    xr,
    ys,
    yr,
    wq0,
    wo,
    acc,
    key_rows,
    query_sum,
    ones,
    lat_sem,
    gain_sem,
    wq_sem,
    wo_sem,
    s1,
    r1,
    s2,
    r2,
    ready,
):
    rows, columns, model = lat_hbm.shape
    places = rows * columns // (n * CHUNKS)
    tokens = n * places
    half_rows = rows // CHUNKS
    groups = len(MID_CUTS) - 1
    pairs = HEADS // 2
    me = lax.axis_index("frame")
    planes = n // PLANE
    depth = lax.div(me, PLANE)
    spot = lax.rem(me, PLANE)
    turn = [lax.rem(spot + k, PLANE) for k in range(PLANE)]
    ascending = [k + (me <= k).astype(jnp.int32) for k in range(n - 1)]

    def tell(semaphore, to):
        pl.semaphore_signal(semaphore, inc=1, device_id={"frame": to}, device_id_type=MESH)

    lat_loads = []
    for c in range(CHUNKS):
        part = pl.ds(c * half_rows, half_rows)
        lat_loads.append(pltpu.make_async_copy(lat_hbm.at[part], lat.at[part], lat_sem.at[c]))
    gains = [
        pltpu.make_async_copy(src, dst, gain_sem.at[i])
        for i, (src, dst) in enumerate(((ln_hbm, ln_ref), (qg_hbm, qg_ref), (kg_hbm, kg_ref)))
    ]
    for load in (lat_loads[0], gains[0], lat_loads[1], gains[1], gains[2]):
        load.start()

    for plane in range(planes - 1, 0, -1):

        @pl.when(depth < plane)
        def _():
            for t in turn:
                tell(pltpu.get_barrier_semaphore(), plane * PLANE + t)

    for k in range(1, PLANE):

        @pl.when(spot + k < PLANE)
        def _():
            tell(pltpu.get_barrier_semaphore(), me + k)

    wq_parts = (wq0,)
    wq_loads = []
    for g in range(groups):
        a, b = MID_CUTS[g], MID_CUTS[g + 1]
        for third in range(3):
            load = pltpu.make_async_copy(
                wq_hbm.at[:, pl.ds(third * model + a, b - a)],
                wq_parts[g].at[:, pl.ds(third * (b - a), b - a)],
                wq_sem.at[g, third],
            )
            wq_loads.append(load)
    load_out = pltpu.make_async_copy(wo_hbm, wo, wo_sem)

    def send_all(src, dst, send, recv, a, b, order):
        for to in order:
            pltpu.make_async_remote_copy(
                src_ref=src.at[to, :, pl.ds(a, b - a)],
                dst_ref=dst.at[me, :, pl.ds(a, b - a)],
                send_sem=send,
                recv_sem=recv,
                device_id={"frame": to},
                device_id_type=MESH,
            ).start()

    def all_copies(src, dst, send, recv, a, b):
        return pltpu.make_async_remote_copy(
            src_ref=src.at[pl.ds(0, n - 1), :, pl.ds(a, b - a)],
            dst_ref=dst.at[pl.ds(0, n - 1), :, pl.ds(a, b - a)],
            send_sem=send,
            recv_sem=recv,
            device_id={"frame": ascending[0]},
            device_id_type=MESH,
        )

    def normalize(c):
        lat_loads[c].wait()
        block = lat[c * half_rows : (c + 1) * half_rows]
        values = block.astype(F32).reshape(tokens, model)
        center = values - jnp.mean(values, axis=-1, keepdims=True)
        spread = jnp.mean(center * center, axis=-1, keepdims=True)
        normed = center * lax.rsqrt(spread + 1e-06) * ln_ref[...].reshape(1, model)
        xs[c] = normed.reshape(n, places, model).astype(BF16)

    def send_normed(c, order):
        send_all(xs.at[c], xr.at[c], s1.at[c], r1.at[c], 0, model, order)

    @pl.when(me > 0)
    def _():
        pl.semaphore_wait(pltpu.get_barrier_semaphore(), me)

    for plane in range(planes - 1):

        @pl.when(plane < depth)
        def _():
            for t in turn:
                tell(ready.at[depth], plane * PLANE + t)

    for k in range(1, PLANE):

        @pl.when(spot >= k)
        def _():
            tell(ready.at[depth], me - k)

    gains[0].wait()
    normalize(0)
    for plane in range(planes):
        if plane == planes - 1:
            normalize(1)
        missing = jnp.where(plane > depth, PLANE, jnp.where(plane == depth, PLANE - 1 - spot, 0))

        @pl.when(missing > 0)
        def _():
            pl.semaphore_wait(ready.at[plane], missing)

        @pl.when(plane != depth)
        def _():
            send_normed(0, [plane * PLANE + turn[0]])

        send_normed(0, [plane * PLANE + t for t in turn[1:]])
    send_normed(1, [lax.rem(me + k, n) for k in range(1, n)])
    for load in wq_loads:
        load.start()
    load_out.start()
    for c in range(CHUNKS):
        xr[c, pl.ds(me, 1)] = xs[c, pl.ds(me, 1)]

    gains[1].wait()
    gains[2].wait()
    entry = lax.broadcasted_iota(jnp.int32, (HEAD_DIM, model), 0)
    place = lax.broadcasted_iota(jnp.int32, (HEAD_DIM, model), 1)
    repeat = (lax.rem(place, HEAD_DIM) == entry).astype(F32)
    both = qg_ref[...] * kg_ref[...] * (HEAD_DIM**-0.5 * LOG2_E)
    gain = jnp.dot(
        jnp.broadcast_to(both.reshape(1, HEAD_DIM), (8, HEAD_DIM)),
        repeat,
        preferred_element_type=F32,
        precision=lax.Precision.HIGHEST,
    )[0:1]

    def head_of(shape, axis, p):
        lane = lax.broadcasted_iota(jnp.int32, shape, axis) + (p * LANES - 2 * p * HEAD_DIM)
        return jnp.where(lane < 0, -1, jnp.where(lane < HEAD_DIM, 0, jnp.where(lane < 2 * HEAD_DIM, 1, 2)))

    def one_zero(mask):
        return jnp.where(mask, 1.0, 0.0).astype(BF16)

    for p in range(pairs):
        down = head_of((WINDOW, 1), 0, p)
        over = head_of((1, WINDOW), 1, p)
        key_rows[p] = one_zero(lax.broadcasted_iota(jnp.int32, (KEY_ROWS, 1), 0) == over)
        slot = lax.div(lax.broadcasted_iota(jnp.int32, (1, 2 * tokens), 1), tokens)
        query_sum[p] = one_zero(down == slot)
        slot = lax.div(lax.broadcasted_iota(jnp.int32, (2 * tokens, 1), 0), tokens)
        ones[p] = one_zero(slot == over)
    row_i = lax.broadcasted_iota(jnp.int32, (tokens, 2 * tokens), 0)
    col_i = lax.broadcasted_iota(jnp.int32, (tokens, 2 * tokens), 1)
    same = lax.rem(row_i, places) == lax.rem(col_i, places)

    for c in range(CHUNKS):
        carry = None
        for g in range(groups):
            a, b = MID_CUTS[g], MID_CUTS[g + 1]
            if c == 0:
                for load in wq_loads[3 * g : 3 * g + 3]:
                    load.wait()
            if g == 0:
                all_copies(xs.at[c], xr.at[c], s1.at[c], r1.at[c], 0, model).wait_recv()
                part = xr[c].astype(F32).reshape(tokens, model).astype(BF16)
            weights = wq_parts[g]
            width = b - a
            for col in range(0, 3 * width, STEP):
                end = min(col + STEP, 3 * width)
                product = jnp.dot(part, weights[:, col:end], preferred_element_type=F32)
                for tile in range(col, end, LANES):
                    to = tile // width * model + a + tile % width
                    acc[:, to : to + LANES] = product[:, tile - col : tile - col + LANES]

            span = range(PAIR_CUTS[g], PAIR_CUTS[g + 1])
            k_sums, q_sums, scores, probs, tops, totals = {}, {}, {}, {}, {}, {}
            for p in span:
                lo, hi = p * LANES, p * LANES + WINDOW
                query = acc[:, lo:hi]
                keys = acc[:, model + lo : model + hi]
                sums = lax.dot_general(
                    key_rows[p],
                    (keys * keys).astype(BF16),
                    (((1,), (1,)), ((), ())),
                    preferred_element_type=F32,
                )
                k_sums[p] = jnp.concatenate([sums[0:1], sums[1:2]], axis=1)
                q_sums[p] = jnp.dot(
                    (query * query).astype(BF16), query_sum[p], preferred_element_type=F32
                )
            for p in span:
                lo, hi = p * LANES, p * LANES + WINDOW
                over = head_of((1, WINDOW), 1, p)
                keys = acc[:, model + lo : model + hi]
                keys = keys * gain[:, lo:hi]
                keys = jnp.concatenate(
                    [jnp.where(over == 0, keys, 0.0), jnp.where(over == 1, keys, 0.0)], axis=0
                ).astype(BF16)
                scores[p] = lax.dot_general(
                    acc[:, lo:hi].astype(BF16),
                    keys,
                    (((1,), (1,)), ((), ())),
                    preferred_element_type=F32,
                )
            for p in span:
                scaled = scores[p] * lax.rsqrt(q_sums[p] * (1.0 / HEAD_DIM) + 1e-06)
                scaled = scaled * lax.rsqrt(k_sums[p] * (1.0 / HEAD_DIM) + 1e-06)
                probs[p] = jnp.where(same, jnp.exp2(scaled), 0.0).astype(BF16)
            for p in span:
                lo, hi = p * LANES, p * LANES + WINDOW
                over = head_of((1, WINDOW), 1, p)
                vals = acc[:, 2 * model + lo : 2 * model + hi]
                vals = jnp.concatenate(
                    [jnp.where(over == 0, vals, 0.0), jnp.where(over == 1, vals, 0.0)], axis=0
                ).astype(BF16)
                tops[p] = jnp.dot(probs[p], vals, preferred_element_type=F32)
                totals[p] = jnp.dot(probs[p], ones[p], preferred_element_type=F32)
            for p in span:
                lo = p * LANES
                top, total = tops[p][:, :LANES], totals[p][:, :LANES]
                if carry is not None:
                    top, total = top + carry[0], total + carry[1]
                ys[c, :, :, lo : lo + LANES] = (top / total).reshape(n, places, LANES).astype(BF16)
                carry = (tops[p][:, LANES:], totals[p][:, LANES:])
            if g == groups - 1:
                done = carry[0] / carry[1]
                ys[c, :, :, model - LANES :] = done.reshape(n, places, LANES).astype(BF16)
            a, b = OUT_CUTS[g], OUT_CUTS[g + 1]
            send_all(ys.at[c], yr.at[c], s2.at[c, g], r2.at[c, g], a, b, ascending if c else [lax.rem(me + k, n) for k in range(1, n)])
        yr[c, pl.ds(me, 1)] = ys[c, pl.ds(me, 1)]

    load_out.wait()
    for c in range(CHUNKS):
        all_copies(xs.at[c], xr.at[c], s1.at[c], r1.at[c], 0, model).wait_send()
    for c in range(CHUNKS):
        piece = pl.ds(c * half_rows, half_rows)
        branch = lat[c * half_rows : (c + 1) * half_rows].astype(F32).reshape(tokens, model)
        for g in range(groups):
            a, b = OUT_CUTS[g], OUT_CUTS[g + 1]
            all_copies(ys.at[c], yr.at[c], s2.at[c, g], r2.at[c, g], a, b).wait_recv()
            part = yr[c, :, :, a:b].astype(F32).reshape(tokens, b - a).astype(BF16)
            product = jnp.dot(part, wo[a:b, :], preferred_element_type=F32)
            out_ref[piece] = (branch + product).reshape(half_rows, columns, model).astype(BF16)
    for c in range(CHUNKS):
        for g in range(groups):
            a, b = OUT_CUTS[g], OUT_CUTS[g + 1]
            all_copies(ys.at[c], yr.at[c], s2.at[c, g], r2.at[c, g], a, b).wait_send()


def fused(n, latent, ln_gain, q_gain, k_gain, w_qkv, w_out):
    rows, columns, model = latent.shape
    places = rows * columns // (n * CHUNKS)
    tokens = n * places
    vmem = pl.BlockSpec(memory_space=pltpu.VMEM)
    hbm = pl.BlockSpec(memory_space=pltpu.HBM)
    block = pltpu.VMEM((CHUNKS, n, places, model), BF16)
    groups = len(MID_CUTS) - 1
    pairs = HEADS // 2
    dma = pltpu.SemaphoreType.DMA
    return pl.pallas_call(
        functools.partial(kernel, n),
        out_shape=jax.ShapeDtypeStruct(latent.shape, BF16),
        in_specs=[hbm] * 6,
        out_specs=vmem,
        scratch_shapes=[
            pltpu.VMEM(latent.shape, BF16),
            pltpu.VMEM(ln_gain.shape, F32),
            pltpu.VMEM(q_gain.shape, F32),
            pltpu.VMEM(k_gain.shape, F32),
            block,
            block,
            block,
            block,
            pltpu.VMEM((model, 3 * (MID_CUTS[1] - MID_CUTS[0])), BF16),
            pltpu.VMEM(w_out.shape, BF16),
            pltpu.VMEM((tokens, w_qkv.shape[1]), F32),
            pltpu.VMEM((pairs, KEY_ROWS, WINDOW), BF16),
            pltpu.VMEM((pairs, WINDOW, 2 * tokens), BF16),
            pltpu.VMEM((pairs, 2 * tokens, WINDOW), BF16),
            dma((CHUNKS,)),
            dma((3,)),
            dma((groups, 3)),
            dma,
            dma((CHUNKS,)),
            dma((CHUNKS,)),
            dma((CHUNKS, groups)),
            dma((CHUNKS, groups)),
            pltpu.SemaphoreType.REGULAR((n // PLANE,)),
        ],
        compiler_params=pltpu.CompilerParams(
            collective_id=0, has_side_effects=True, vmem_limit_bytes=VMEM_BYTES
        ),
    )(
        *(
            pltpu.with_memory_space_constraint(value, pltpu.HBM)
            for value in (latent, ln_gain, q_gain, k_gain, w_qkv, w_out)
        )
    )


def layer_norm(rows, ln_gain):
    values = rows.astype(jnp.float32)
    center = values - jnp.mean(values, axis=-1, keepdims=True)
    spread = jnp.mean(center * center, axis=-1, keepdims=True)
    return (center * lax.rsqrt(spread + 1e-06) * ln_gain).astype(jnp.bfloat16)


def head_norm(values, gain):
    shaped = values.reshape(values.shape[:-1] + (HEADS, HEAD_DIM))
    mean_sq = jnp.mean(shaped * shaped, axis=-1, keepdims=True)
    return (shaped * lax.rsqrt(mean_sq + 1e-06) * gain).astype(jnp.bfloat16).reshape(values.shape)


def project(normed, w_qkv, q_gain, k_gain):
    width = normed.shape[-1]
    mixed = jnp.dot(normed.reshape(-1, width), w_qkv, preferred_element_type=jnp.float32)
    mixed = mixed.reshape(normed.shape[:-1] + (3 * width,))
    query = head_norm(mixed[..., :width], q_gain)
    keys = head_norm(mixed[..., width : 2 * width], k_gain)
    values = mixed[..., 2 * width :].astype(jnp.bfloat16)
    return (query, keys, values)


def attend(query, keys, values):
    lead = query.shape[0]
    others = query.shape[1]
    q_four = query.reshape(lead, others, HEADS, HEAD_DIM)
    k_four = keys.reshape(lead, others, HEADS, HEAD_DIM)
    v_four = values.reshape(lead, others, HEADS, HEAD_DIM)
    scores = jnp.einsum(
        "tshe,ushe->shtu", q_four, k_four, preferred_element_type=jnp.float32
    ) * HEAD_DIM ** (-0.5)
    weights = jnp.exp(scores)
    weights = (weights / jnp.sum(weights, axis=-1, keepdims=True)).astype(jnp.bfloat16)
    mixed = jnp.einsum("shtu,ushe->tshe", weights, v_four, preferred_element_type=jnp.float32)
    return mixed.astype(jnp.bfloat16).reshape(query.shape)


def body(latent, ln_gain, q_gain, k_gain, w_qkv, w_out):
    device_count = lax.axis_size("frame")
    rows, columns, model = latent.shape
    positions = rows * columns
    per_peer = positions // device_count
    if per_peer % 8 == 0 and rows % CHUNKS == 0 and device_count % PLANE == 0:
        return fused(device_count, latent, ln_gain, q_gain, k_gain, w_qkv, w_out)
    flat = latent.reshape(positions, model)
    normed = layer_norm(flat, ln_gain)
    query, keys, values = project(
        lax.all_to_all(
            normed.reshape(device_count, per_peer, model),
            "frame",
            split_axis=0,
            concat_axis=0,
            tiled=True,
        ),
        w_qkv,
        q_gain,
        k_gain,
    )
    mixed = attend(query, keys, values)
    returned = lax.all_to_all(mixed, "frame", split_axis=0, concat_axis=0, tiled=True)
    attended = returned.reshape(positions, model)
    branch = jnp.dot(attended, w_out, preferred_element_type=jnp.float32)
    result = flat.astype(jnp.float32) + branch
    return result.astype(jnp.bfloat16).reshape(latent.shape)


def solution(mesh):
    placed = (P(("groups", "frame"), None, None), P(), P(), P(), P(), P())
    return jax.shard_map(
        body,
        mesh=mesh,
        in_specs=placed,
        out_specs=P(("groups", "frame"), None, None),
        check_vma=False,
    )
```
